256 devices in a mesh: px: 8 (over z_hi, y), py: 32 (over x, z_lo, core).
Axes of the slice: x: 4, y: 4, z: 8 (z_hi: 2, z_lo: 4; z = z_hi * 4 + z_lo), core: 2. Of those that a mesh axis runs over, the one named last changes fastest.
Arguments:
- velocity: float32 [3, 128, 128, 128], P(None, 'px', 'py'), may hold values from -4 to 4
- cotangent: float32 [3, 128, 128, 128], P(None, 'px', 'py'), may hold values from -6 to 6
- weight_in: bfloat16 [32, 3, 3, 3, 3], replicated, may hold values from -0.625 to 0.625
- bias_in: float32 [32], replicated, may hold values from -3 to 3
- weight_out: bfloat16 [6, 32, 3, 3, 3], replicated, may hold values from -0.21875 to 0.21875
Outputs:
- adjoint: float32 [3, 128, 128, 128], P(None, 'px', 'py')
The draws below stay inside these ranges and needn't reach their ends.
All inputs are finite; a program needn't handle non-finite values.
Results may differ from the reference program's by a relative error of at most 0.00041.
Values sent between devices are 32-bit elements; how exact they have to be, the bound alone decides.
No kernel may reach another device: no remote copies, remote signals or barrier semaphores. Data moves between devices by JAX's collectives and lax.ppermute only.
A program may use at most 64 MiB of HBM per device.

```python
import math
import jax
import jax.numpy as jnp
from jax import lax

NX = 128
NY = 128
NZ = 128
HID = 32
COMP = 3
STRESS = 6
KS = 3


def block_levels(stream_key, dims, split, smallest, largest):
    factor_of = 1.0
    for axis_at, parts in split:
        steps = jax.random.uniform(jax.random.fold_in(jax.random.fold_in(stream_key, 6), axis_at), (parts,), jnp.float32, smallest / len(split), largest / len(split))
        factor_of = factor_of * jnp.repeat(jnp.exp(steps), dims[axis_at] // parts).reshape((-1,) + (1,) * (len(dims) - 1 - axis_at))
    return factor_of


def noise(own_key, shape, spread, reach, cuts=(), kind=jnp.bfloat16):
    values = spread * jax.random.normal(own_key, shape, jnp.float32)
    if cuts:
        values = values * block_levels(own_key, shape, cuts, -0.22, 0.18)
    return jnp.clip(values, -reach, reach).astype(kind)


def setup_inputs(seed: int = 0) -> dict:
    seeds = jax.random.split(jax.random.key(seed), 6)
    return {
        "velocity": noise(seeds[0], (COMP, NX, NY, NZ), 1.0, 4.0, ((1, 8), (2, 32)), jnp.float32),
        "cotangent": noise(seeds[1], (COMP, NX, NY, NZ), 1.0, 6.0, ((1, 8), (2, 32)), jnp.float32),
        "weight_in": noise(seeds[2], (HID, COMP, KS, KS, KS), (COMP * KS * KS * KS) ** -0.5, 0.625),
        "bias_in": noise(seeds[3], (HID,), 1.0, 3.0, (), jnp.float32),
        "weight_out": noise(seeds[4], (STRESS, HID, KS, KS, KS), (HID * KS * KS * KS) ** -0.5, 0.21875),
    }


time_step = 0.005


def shifted(source, spatial, offset, margin):
    slicers = [slice(None)]
    for position in range(1, 4):
        extent = source.shape[position]
        offset_now = offset if position == spatial else 0
        slicers.append(slice(margin + offset_now, extent - margin + offset_now))
    return source[tuple(slicers)]


def central(source, spatial, spacing):
    return (shifted(source, spatial, 1, 1) - shifted(source, spatial, -1, 1)) / (2.0 * spacing)


def sixth_order(source, spatial, spacing):
    first = shifted(source, spatial, 1, 3) - shifted(source, spatial, -1, 3)
    second = shifted(source, spatial, 2, 3) - shifted(source, spatial, -2, 3)
    third = shifted(source, spatial, 3, 3) - shifted(source, spatial, -3, 3)
    return (45.0 * first - 9.0 * second + third) / (60.0 * spacing)


def correlate(source, kernel):
    result = lax.conv_general_dilated(source[None], kernel, (1, 1, 1), "VALID",
                                      dimension_numbers=("NCDHW", "OIDHW", "NCDHW"),
                                      preferred_element_type=jnp.float32)
    return result[0]


def step_adjoint(vel_ext, lam_ext, weight_in, bias_in, weight_out, spacings):
    low_velocity = vel_ext[:, 1:-1, 1:-1, 1:-1].astype(jnp.bfloat16)
    pre_act = correlate(low_velocity, weight_in) + bias_in[:, None, None, None]
    tanh_slope = 1.0 - jnp.square(jnp.tanh(pre_act))
    lam_grads = [[central(lam_ext[component:component + 1], direction + 1, spacings[direction])[0]
                  for direction in range(3)] for component in range(3)]
    stress_adj = jnp.stack([lam_grads[0][0], lam_grads[1][1], lam_grads[2][2],
                            lam_grads[0][1] + lam_grads[1][0],
                            lam_grads[0][2] + lam_grads[2][0],
                            lam_grads[1][2] + lam_grads[2][1]]).astype(jnp.bfloat16)
    kernel_out = jnp.flip(weight_out, (2, 3, 4)).transpose(1, 0, 2, 3, 4)
    hidden_adj = correlate(stress_adj, kernel_out)
    pre_adj = (hidden_adj * tanh_slope).astype(jnp.bfloat16)
    kernel_in = jnp.flip(weight_in, (2, 3, 4)).transpose(1, 0, 2, 3, 4)
    closure_adj = correlate(pre_adj, kernel_in)
    lam_block = lam_ext[:, 3:-3, 3:-3, 3:-3]
    advect = sixth_order(lam_ext * vel_ext[0:1], 1, spacings[0])
    for direction in range(1, 3):
        advect = advect + sixth_order(lam_ext * vel_ext[direction:direction + 1], direction + 1, spacings[direction])
    cross_terms = jnp.stack([jnp.sum(lam_block * sixth_order(vel_ext, direction + 1, spacings[direction]), axis=0)
                             for direction in range(3)])
    advect = advect - cross_terms
    return lam_block + time_step * (advect + closure_adj)


def reference(velocity, cotangent, weight_in, bias_in, weight_out):
    spectrum = jnp.fft.fftn(cotangent, axes=(1, 2, 3))
    wave_x = (jnp.fft.fftfreq(NX) * NX)[:, None, None]
    wave_y = (jnp.fft.fftfreq(NY) * NY)[None, :, None]
    wave_z = (jnp.fft.fftfreq(NZ) * NZ)[None, None, :]
    retain = ((wave_x != -(NX // 2)) & (wave_y != -(NY // 2)) & (wave_z != -(NZ // 2)))
    squared = wave_x * wave_x + wave_y * wave_y + wave_z * wave_z
    inverse = jnp.where(squared > 0, 1.0 / jnp.maximum(squared, 1.0), 0.0)
    dotted = (wave_x * spectrum[0] + wave_y * spectrum[1] + wave_z * spectrum[2]) * inverse
    projected = jnp.stack([spectrum[0] - wave_x * dotted,
                           spectrum[1] - wave_y * dotted,
                           spectrum[2] - wave_z * dotted]) * retain[None]
    lam = jnp.real(jnp.fft.ifftn(projected, axes=(1, 2, 3))).astype(jnp.float32)
    widths = ((0, 0), (3, 3), (3, 3), (3, 3))
    vel_pad = jnp.pad(velocity, widths, mode="wrap")
    lam_pad = jnp.pad(lam, widths, mode="wrap")
    spacings = (2.0 * math.pi / NX, 2.0 * math.pi / NY, 2.0 * math.pi / NZ)
    slab_width = math.gcd(NX, 16)
    slab_count = NX // slab_width

    def one_slab(slab_index):
        slab_start = (slab_index * slab_width).astype(jnp.int32)
        vel_slab = lax.dynamic_slice_in_dim(vel_pad, slab_start, slab_width + 6, 1)
        lam_slab = lax.dynamic_slice_in_dim(lam_pad, slab_start, slab_width + 6, 1)
        return step_adjoint(vel_slab, lam_slab, weight_in, bias_in, weight_out, spacings)

    pieces = lax.map(one_slab, jnp.arange(slab_count, dtype=jnp.int32))
    return pieces.transpose(1, 0, 2, 3, 4).reshape(COMP, NX, NY, NZ)
```

```python
import functools
import math

import jax
import jax.numpy as jnp
import ml_dtypes
import numpy as np
from jax import lax
from jax.experimental import pallas as pl
from jax.experimental.pallas import tpu as pltpu
from jax.sharding import PartitionSpec as P

N = 128
PX = 8
PY = 32
time_step = 0.005
spacing = 2.0 * math.pi / N
bf16 = jnp.bfloat16
f32 = jnp.float32
PRE = 80
STR = 144


def halves(table):
    table = np.asarray(table, np.float64)
    high = table.astype(np.float32).astype(ml_dtypes.bfloat16)
    low = (table - high.astype(np.float64)).astype(np.float32).astype(ml_dtypes.bfloat16)
    return np.stack([high, low])


def complex_form(table):
    return np.block([[table.real, table.imag], [-table.imag, table.real]])


@functools.cache
def constants():
    z = np.arange(N)
    kz = np.arange(N // 2)
    angle = 2 * np.pi * ((kz[:, None] * z[None]) % N) / N
    cos, sin = np.cos(angle), np.sin(angle)
    weight = np.where(kz == 0, 1.0, 2.0)[:, None] / float(N) ** 3

    def pair(first, second):
        return np.stack([first, second], 1).reshape(N, N)

    forward_z = np.stack([halves(pair(cos, -sin)), halves(pair(sin, cos))])
    backward_z = np.stack(
        [halves(pair(cos * weight, -sin * weight)), halves(pair(sin * weight, cos * weight))]
    )
    a, b = np.arange(PX), np.arange(PY)
    y4, x16 = np.arange(4), np.arange(16)
    phase = a[:, None, None, None] * a[None, None, :, None] / PX
    phase = phase + b[None, :, None, None] * b[None, None, None, :] / PY
    rows = np.exp(-2j * np.pi * phase.reshape(256, 256))
    row_forward = halves(np.concatenate([rows.real, rows.imag], 0))
    row_backward = halves(np.concatenate([rows.real, rows.imag], 1))
    phase = a[:, None, None, None] * x16 + b[None, :, None, None] * y4[:, None]
    twiddle = np.exp(-2j * np.pi * phase.reshape(256, 64) / N)
    twiddle = np.tile(twiddle, (1, 2))
    twiddle = np.stack([twiddle.real, twiddle.imag]).astype(np.float32)
    phase = y4[:, None, None, None] * y4[:, None] / 4 + x16[:, None, None] * x16 / 16
    lanes = np.exp(-2j * np.pi * phase.reshape(64, 64))
    lane_forward = halves(complex_form(np.kron(np.eye(2), lanes)))
    m, l = np.broadcast_arrays(
        a[:, None, None, None] + 8 * x16, b[None, :, None, None] + 32 * y4[:, None]
    )
    m, l = m.reshape(256, 64), l.reshape(256, 64)
    kx, ky = np.where(m > 64, m - N, m), np.where(l > 64, l - N, l)
    square = np.tile(kx * kx + ky * ky, (1, 2))
    retain = np.tile((m != 64) & (l != 64), (1, 2))
    waves = np.stack([np.concatenate([kx, ky], 1), square, retain]).astype(np.float32)
    r = np.arange(24)
    xe = np.where(r < 19, r, r - 24)
    lane_backward, twiddle_back = [], []
    for part in range(2):
        ye = np.arange(5) + (5 * part - 3)
        phase = y4[:, None, None, None] * ye[:, None] / 4 + x16[:, None, None] * xe / 16
        table = np.pad(np.exp(2j * np.pi * phase.reshape(64, 120)), ((0, 0), (0, 8)))
        for component in range(2):
            pick = np.eye(2)[:, component : component + 1]
            lane_backward.append(halves(complex_form(np.kron(pick, table))))
        phase = a[:, None, None, None] * xe + b[None, :, None, None] * ye[:, None]
        table = np.pad(np.exp(2j * np.pi * phase.reshape(256, 120) / N), ((0, 0), (0, 8)))
        twiddle_back.append(np.stack([table.real, table.imag]))
    lane_backward = np.stack(lane_backward).reshape(2, 2, 2, 256, 256)
    twiddle_back = np.stack(twiddle_back).astype(np.float32)
    select_in = np.zeros((3, 3, 3, 3, 3 * PRE))
    select_out = np.zeros((6, 3, 3, 3, 3 * STR))
    select_back = np.zeros((3, 6, 3, 16, 3, 3, 3, 3))
    for dx in range(3):
        for dz in range(3):
            for dy in range(3):
                for c in range(3):
                    select_in[c, dx, dy, dz, dx * PRE + dz * 24 + c * 8 + dy] = 1
                for s in range(6):
                    column = dx * STR + dz * 48 + s * 8 + dy
                    select_out[s, 2 - dx, 2 - dy, 2 - dz, column] = 1
            for c in range(3):
                for yo in range(4):
                    for yi in range(6):
                        if 0 <= yo + 2 - yi < 3:
                            select_back[dx, yi, dz, c * 4 + yo, c, 2 - dx, yo + 2 - yi, dz] = 1
    select_in = select_in.reshape(81, 3 * PRE).astype(ml_dtypes.bfloat16)
    select_out = select_out.reshape(162, 3 * STR).astype(ml_dtypes.bfloat16)
    select_back = select_back.reshape(18 * 48, 81).astype(ml_dtypes.bfloat16)
    return dict(
        forward_z=forward_z,
        backward_z=backward_z,
        row_forward=row_forward,
        row_backward=row_backward,
        twiddle=twiddle,
        lane_forward=lane_forward,
        waves=waves,
        lane_backward=lane_backward,
        twiddle_back=twiddle_back,
        select_in=select_in,
        select_out=select_out,
        select_back=select_back,
    )


def split(value):
    high = value.astype(bf16)
    return high, (value - high.astype(f32)).astype(bf16)


def product(left, right, over=(1, 0)):
    dims = (((over[0],), (over[1],)), ((), ()))

    def one(a, b):
        return lax.dot_general(a, b, dims, preferred_element_type=f32)

    return one(left[0], right[0]) + (one(left[1], right[0]) + one(left[0], right[1]))


def transform_z(source, table, out):
    blocks = [[source[pl.ds(c * 64 + y, 16, stride=4), :] for y in range(4)] for c in range(3)]
    first = jnp.concatenate(blocks[0] + blocks[1], 0)
    second = jnp.concatenate(blocks[2] + blocks[2], 0)
    for tile, cells in enumerate((first, second)):
        modes = product((table[tile, 0], table[tile, 1]), split(cells), (1, 1))
        for copy in range(2):
            out[pl.ds(2 * copy + tile, 128, stride=4), :] = modes


def project(
    which,
    source,
    row_forward,
    twiddle,
    lane_forward,
    waves,
    lane_backward,
    twiddle_back,
    row_backward,
    out,
):
    part = which[0]
    kz = which[1].astype(f32)
    tiles = [source[pl.ds(tile, 256, stride=2), :] for tile in range(2)]
    mixed = product((row_forward[0], row_forward[1]), split(jnp.concatenate(tiles, 1)))
    cos, sin = twiddle[0], twiddle[1]
    spectrum = []
    for tile in range(2):
        real = mixed[:256, tile * 128 : tile * 128 + 128]
        imag = mixed[256:, tile * 128 : tile * 128 + 128]
        turned = jnp.concatenate([real * cos - imag * sin, real * sin + imag * cos], 1)
        spectrum.append(product(split(turned), (lane_forward[0], lane_forward[1])))
    wave, square, retain = waves[0], waves[1], waves[2]
    inverse = 1.0 / jnp.maximum(square + kz * kz, 1.0)
    (hr, hi), (vr, vi) = [(s[:, :128], s[:, 128:]) for s in spectrum]
    flat_r, flat_i = hr * wave, hi * wave
    flat_r = flat_r + pltpu.roll(flat_r, 64, 1)
    flat_i = flat_i + pltpu.roll(flat_i, 64, 1)
    dot_r = (flat_r + kz * vi) * inverse
    dot_i = (flat_i - kz * vr) * inverse
    flat = jnp.concatenate([(hr - wave * dot_r) * retain, (hi - wave * dot_i) * retain], 1)
    upright = jnp.concatenate([(vr + kz * dot_i) * retain, (vi - kz * dot_r) * retain], 1)
    flat, upright = split(flat), split(upright)
    cos, sin = twiddle_back[part, 0], twiddle_back[part, 1]
    parts = []
    for component in range(3):
        matrix = lane_backward.at[part, component % 2]
        cells = product(upright if component == 2 else flat, (matrix[0], matrix[1]))
        real, imag = cells[:, :128], cells[:, 128:]
        parts.append(jnp.concatenate([real * cos - imag * sin, real * sin + imag * cos], 0))
    result = product((row_backward[0], row_backward[1]), split(jnp.concatenate(parts, 1)))
    for component in range(3):
        block = result[:, component * 128 : component * 128 + 128]
        out[pl.ds(component, 256, stride=3), :] = block


def extend_x(source, low, high, out):
    for c in range(3):
        for y in range(4):
            base = (c * 4 + y) * 24
            out[pl.ds(base + 16, 8), :] = jnp.zeros((8, 128), f32)
            out[pl.ds(base, 16), :] = source[pl.ds(c * 64 + y, 16, stride=4), :]
            out[pl.ds(base + 16, 3), :] = high[pl.ds(c * 12 + y, 3, stride=4), :]
            out[pl.ds(base + 21, 3), :] = low[pl.ds(c * 12 + y, 3, stride=4), :]


def sixth(at):
    near, middle, far = [at(k) - at(-k) for k in (1, 2, 3)]
    return (45.0 * near - 9.0 * middle + far) * (1.0 / (60.0 * spacing))


def rolled(block, axis):
    return lambda k: pltpu.roll(block, (-k) % block.shape[axis], axis)


def prepare(
    own,
    low,
    high,
    kernel_in,
    kernel_out,
    bias,
    select_in,
    select_out,
    select_back,
    field,
    slope,
    slants,
    banded_out,
    banded_back,
    banded_in,
    slabs,
):
    for c in range(3):
        field[pl.ds(c * 240, 72), :] = low[pl.ds(c * 72, 72), :]
        field[pl.ds(c * 240 + 72, 96), :] = own[pl.ds(c * 96, 96), :]
        field[pl.ds(c * 240 + 168, 72), :] = high[pl.ds(c * 72, 72), :]
    over_rows = (((0,), (0,)), ((), ()))
    band = lax.dot_general(kernel_in[...], select_in[...], over_rows, preferred_element_type=f32)
    for yo in range(6):
        moved = band if yo == 0 else jnp.concatenate([jnp.zeros((32, yo), f32), band[:, :-yo]], 1)
        banded_in[pl.ds(yo * 32, 32), :] = moved.astype(bf16)
    band = lax.dot_general(kernel_out[...], select_out[...], over_rows, preferred_element_type=f32)
    for yo in range(6):
        moved = band if yo == 0 else jnp.concatenate([jnp.zeros((32, yo), f32), band[:, :-yo]], 1)
        banded_out[pl.ds(yo * 32, 32), :] = moved.astype(bf16)
    band = jnp.dot(select_back[...], kernel_in[...], preferred_element_type=f32).astype(bf16)
    for block in range(18):
        banded_back[:, pl.ds(block * 32, 32)] = band[block * 48 : block * 48 + 48]

    def gather(i, carry):
        row = lax.rem(i + 22, 24)
        parts = [field[pl.ds(c * 240 + 24 + row, 8, stride=24), :] for c in range(3)]
        slab = jnp.concatenate(parts, 0)
        shifts = [pltpu.roll(slab, 1, 1), slab, pltpu.roll(slab, 127, 1)]
        slab = jnp.concatenate(shifts + [jnp.zeros((8, 128), f32)], 0)
        slabs[pl.ds(pl.multiple_of(i * PRE, 16), PRE), :] = slab.astype(bf16)
        return carry

    lax.fori_loop(0, 20, gather, 0)

    def activate(i, carry):
        cells = slabs[pl.ds(pl.multiple_of(i * PRE, 16), 3 * PRE), :]
        value = jnp.dot(banded_in[...], cells, preferred_element_type=f32) + bias[...]
        value = jnp.tanh(value)
        slope[pl.ds(pl.multiple_of(i * 192, 8), 192), :] = 1.0 - value * value
        return carry

    lax.fori_loop(0, 18, activate, 0)
    for a in range(3):
        for y in range(4):
            base = a * 240 + (y + 3) * 24
            block = field[pl.ds(base, 24), :]
            inner = block[:16]
            along = [
                sixth(rolled(block, 0))[:16],
                sixth(lambda k, base=base: field[pl.ds(base + 24 * k, 16), :]),
                sixth(rolled(inner, 1)),
            ]
            for c in range(3):
                slants[pl.ds(((a * 3 + c) * 4 + y) * 16, 16), :] = along[c]


def finish(
    modes,
    table,
    field,
    slope,
    slants,
    banded_out,
    banded_back,
    out,
    lam,
    stress,
    slabs,
    adjoint,
    closure,
):
    for c in range(3):
        matrix = table.at[c // 2]
        for part in range(2):
            cells = split(modes[pl.ds(part * 3 + c, 128, stride=6), :])
            values = product(cells, (matrix[0], matrix[1]), (0, 0))
            lam[pl.ds(c * 240 + part * 120, 120), :] = values[:120]
    scale = 1.0 / (2.0 * spacing)
    for y in range(8):
        blocks = [lam[pl.ds(c * 240 + (y + 1) * 24, 24), :] for c in range(3)]
        along_x = [(pltpu.roll(b, 23, 0) - pltpu.roll(b, 1, 0)) * scale for b in blocks]
        along_z = [(pltpu.roll(b, 127, 1) - pltpu.roll(b, 1, 1)) * scale for b in blocks]
        along_y = [
            (lam[pl.ds(c * 240 + (y + 2) * 24, 24), :] - lam[pl.ds(c * 240 + y * 24, 24), :]) * scale
            for c in range(3)
        ]
        values = [
            along_x[0],
            along_y[1],
            along_z[2],
            along_y[0] + along_x[1],
            along_z[0] + along_x[2],
            along_z[1] + along_y[2],
        ]
        for s in range(6):
            stress[pl.ds((s * 8 + y) * 24, 24), :] = values[s]

    def gather(i, carry):
        row = lax.rem(i + 22, 24)
        slab = stress[pl.ds(row, 48, stride=24), :]
        shifts = [pltpu.roll(slab, 1, 1), slab, pltpu.roll(slab, 127, 1)]
        slab = jnp.concatenate(shifts, 0)
        slabs[pl.ds(pl.multiple_of(i * STR, 16), STR), :] = slab.astype(bf16)
        return carry

    lax.fori_loop(0, 20, gather, 0)

    def hidden(i, carry):
        cells = slabs[pl.ds(pl.multiple_of(i * STR, 16), 3 * STR), :]
        value = jnp.dot(banded_out[...], cells, preferred_element_type=f32)
        rows = pl.ds(pl.multiple_of(i * 192, 16), 192)
        adjoint[rows, :] = (value * slope[rows, :]).astype(bf16)
        return carry

    lax.fori_loop(0, 18, hidden, 0)

    def back(i, carry):
        cells = adjoint[pl.ds(pl.multiple_of(i * 192, 16), 576), :]
        value = jnp.dot(banded_back[...], cells, preferred_element_type=f32)
        total = value[16:32] + pltpu.roll(value[:16], 127, 1) + pltpu.roll(value[32:], 1, 1)
        closure[pl.ds(pl.multiple_of(i * 16, 16), 16), :] = total
        return carry

    lax.fori_loop(0, 16, back, 0)
    for c in range(3):
        across = [
            lam[pl.ds(c * 240 + y * 24, 16), :] * field[pl.ds(240 + y * 24, 16), :]
            for y in range(10)
        ]
        for y in range(4):
            base = (y + 3) * 24
            block = lam[pl.ds(c * 240 + base, 24), :]
            total = sixth(rolled(block * field[pl.ds(base, 24), :], 0))[:16]
            total = total + sixth(lambda k, y=y: across[y + 3 + k])
            total = total + sixth(rolled(block[:16] * field[pl.ds(480 + base, 16), :], 1))
            crossed = [
                lam[pl.ds(a * 240 + base, 16), :] * slants[pl.ds(((a * 3 + c) * 4 + y) * 16, 16), :]
                for a in range(3)
            ]
            total = total - (crossed[0] + crossed[1] + crossed[2])
            total = total + closure[pl.ds(c * 4 + y, 16, stride=16), :]
            out[pl.ds(c * 64 + y, 16, stride=4), :] = block[:16] + time_step * total


def call(kernel, shapes, args, scratch=(), scalars=0, flops=0):
    size = 4 * sum(math.prod(s.shape) for s in shapes) + 4 * sum(math.prod(a.shape) for a in args)
    whole = pl.BlockSpec(memory_space=pltpu.VMEM)
    return pl.pallas_call(
        kernel,
        out_shape=shapes,
        in_specs=[pl.BlockSpec(memory_space=pltpu.SMEM)] * scalars
        + [whole] * (len(args) - scalars),
        out_specs=[whole] * len(shapes),
        scratch_shapes=list(scratch),
        compiler_params=pltpu.CompilerParams(vmem_limit_bytes=40 * 2**20),
        cost_estimate=pl.CostEstimate(flops=flops, bytes_accessed=size, transcendentals=0),
    )(*args)


def shape(rows, columns=128, kind=f32):
    return jax.ShapeDtypeStruct((rows, columns), kind)


def body(velocity, cotangent, weight_in, bias_in, weight_out):
    t = {name: jnp.asarray(value) for name, value in constants().items()}
    (modes,) = call(
        transform_z, [shape(512)], [cotangent.reshape(192, 128), t["forward_z"]], flops=4 * 2**22
    )
    planes = lax.all_to_all(modes.reshape(256, 256), ("px", "py"), 0, 0, tiled=True)

    up_x = [(i, (i + 1) % PX) for i in range(PX)]
    down_x = [(b, a) for a, b in up_x]
    up_y = [(i, (i + 1) % PY) for i in range(PY)]
    down_y = [(b, a) for a, b in up_y]
    low = lax.ppermute(velocity[:, 13:].reshape(36, 128), "px", up_x)
    high = lax.ppermute(velocity[:, :3].reshape(36, 128), "px", down_x)
    (own,) = call(extend_x, [shape(288)], [velocity.reshape(192, 128), low, high])
    layers = own.reshape(3, 96, 128)
    low = lax.ppermute(layers[:, 24:].reshape(216, 128), "py", up_y)
    high = lax.ppermute(layers[:, :72].reshape(216, 128), "py", down_y)
    kernel_in = weight_in.reshape(32, 81).T
    kernel_out = weight_out.transpose(0, 2, 3, 4, 1).reshape(162, 32)
    bias = jnp.tile(bias_in, 6).reshape(192, 1)
    field, slope, slants, banded_out, banded_back = call(
        prepare,
        [shape(720), shape(18 * 192), shape(576), shape(192, 3 * STR, bf16), shape(48, 576, bf16)],
        [
            own,
            low,
            high,
            kernel_in,
            kernel_out,
            bias,
            t["select_in"],
            t["select_out"],
            t["select_back"],
        ],
        [pltpu.VMEM((192, 3 * PRE), bf16), pltpu.VMEM((20 * PRE, 128), bf16)],
        flops=18 * 2 * 192 * 256 * 128,
    )

    device = lax.axis_index("px") * PY + lax.axis_index("py")
    which = jnp.stack([device % 2, device // 4]).astype(jnp.int32)
    (returned,) = call(
        project,
        [shape(768)],
        [
            which,
            planes.reshape(512, 128),
            t["row_forward"],
            t["twiddle"],
            t["lane_forward"],
            t["waves"],
            t["lane_backward"],
            t["twiddle_back"],
            t["row_backward"],
        ],
        scalars=1,
        flops=30 * 2 * 256**3,
    )
    received = lax.all_to_all(returned.reshape(256, 384), ("px", "py"), 0, 0, tiled=True)
    (result,) = call(
        finish,
        [shape(192)],
        [
            received.reshape(768, 128),
            t["backward_z"],
            field,
            slope,
            slants,
            banded_out,
            banded_back,
        ],
        [
            pltpu.VMEM((720, 128), f32),
            pltpu.VMEM((48 * 24, 128), f32),
            pltpu.VMEM((20 * STR, 128), bf16),
            pltpu.VMEM((18 * 192, 128), bf16),
            pltpu.VMEM((256, 128), f32),
        ],
        flops=2**29,
    )
    return result.reshape(3, 16, 4, 128)


def solution(mesh):
    placed = (P(None, "px", "py", None), P(None, "px", "py", None), P(), P(), P())
    return jax.shard_map(
        body, mesh=mesh, in_specs=placed, out_specs=P(None, "px", "py", None), check_vma=False
    )
```

```python
import functools
import math

import jax
import jax.numpy as jnp
import ml_dtypes
import numpy as np
from jax import lax
from jax.experimental import pallas as pl
from jax.experimental.pallas import tpu as pltpu
from jax.sharding import PartitionSpec as P

N = 128
PX = 8
PY = 32
time_step = 0.005
spacing = 2.0 * math.pi / N
bf16 = jnp.bfloat16
f32 = jnp.float32
FULL = 60 * 2**20
MOST = 2**26 - 9 * 2**15
PRE = 80
STR = 144


def halves(table):
    table = np.asarray(table, np.float64)
    high = table.astype(np.float32).astype(ml_dtypes.bfloat16)
    low = (table - high.astype(np.float64)).astype(np.float32).astype(ml_dtypes.bfloat16)
    return np.stack([high, low])


def complex_form(table):
    return np.block([[table.real, table.imag], [-table.imag, table.real]])


@functools.cache
def constants():
    z = np.arange(N)
    kz = np.arange(N // 2)
    angle = 2 * np.pi * ((kz[:, None] * z[None]) % N) / N
    cos, sin = np.cos(angle), np.sin(angle)
    weight = np.where(kz == 0, 1.0, 2.0)[:, None] / float(N) ** 3

    def pair(first, second):
        return np.stack([first, second], 1).reshape(N, N)

    forward_z = np.stack([halves(pair(cos, -sin)), halves(pair(sin, cos))])
    backward_z = np.stack(
        [halves(pair(cos * weight, -sin * weight)), halves(pair(sin * weight, cos * weight))]
    )
    a, b = np.arange(PX), np.arange(PY)
    y4, x16 = np.arange(4), np.arange(16)
    phase = a[:, None, None, None] * a[None, None, :, None] / PX
    phase = phase + b[None, :, None, None] * b[None, None, None, :] / PY
    rows = np.exp(-2j * np.pi * phase.reshape(256, 256))
    row_forward = halves(np.concatenate([rows.real, rows.imag], 0))
    row_backward = halves(np.concatenate([rows.real, rows.imag], 1))
    phase = a[:, None, None, None] * x16 + b[None, :, None, None] * y4[:, None]
    twiddle = np.exp(-2j * np.pi * phase.reshape(256, 64) / N)
    twiddle = np.tile(twiddle, (1, 2))
    twiddle = np.stack([twiddle.real, twiddle.imag]).astype(np.float32)
    phase = y4[:, None, None, None] * y4[:, None] / 4 + x16[:, None, None] * x16 / 16
    lanes = np.exp(-2j * np.pi * phase.reshape(64, 64))
    lane_forward = halves(complex_form(np.kron(np.eye(2), lanes)))
    m, l = np.broadcast_arrays(
        a[:, None, None, None] + 8 * x16, b[None, :, None, None] + 32 * y4[:, None]
    )
    m, l = m.reshape(256, 64), l.reshape(256, 64)
    kx, ky = np.where(m > 64, m - N, m), np.where(l > 64, l - N, l)
    square = np.tile(kx * kx + ky * ky, (1, 2))
    retain = np.tile((m != 64) & (l != 64), (1, 2))
    waves = np.stack([np.concatenate([kx, ky], 1), square, retain]).astype(np.float32)
    r = np.arange(24)
    xe = np.where(r < 19, r, r - 24)
    lane_backward, twiddle_back = [], []
    for part in range(2):
        ye = np.arange(5) + (5 * part - 3)
        phase = y4[:, None, None, None] * ye[:, None] / 4 + x16[:, None, None] * xe / 16
        table = np.pad(np.exp(2j * np.pi * phase.reshape(64, 120)), ((0, 0), (0, 8)))
        for component in range(2):
            pick = np.eye(2)[:, component : component + 1]
            lane_backward.append(halves(complex_form(np.kron(pick, table))))
        phase = a[:, None, None, None] * xe + b[None, :, None, None] * ye[:, None]
        table = np.pad(np.exp(2j * np.pi * phase.reshape(256, 120) / N), ((0, 0), (0, 8)))
        twiddle_back.append(np.stack([table.real, table.imag]))
    lane_backward = np.stack(lane_backward).reshape(2, 2, 2, 256, 256)
    twiddle_back = np.stack(twiddle_back).astype(np.float32)
    select_in = np.zeros((3, 3, 3, 3, 3 * PRE))
    select_out = np.zeros((6, 3, 3, 3, 3 * STR))
    select_back = np.zeros((3, 6, 3, 16, 3, 3, 3, 3))
    for dx in range(3):
        for dz in range(3):
            for dy in range(3):
                for c in range(3):
                    select_in[c, dx, dy, dz, dx * PRE + dz * 24 + c * 8 + dy] = 1
                for s in range(6):
                    column = dx * STR + dz * 48 + s * 8 + dy
                    select_out[s, 2 - dx, 2 - dy, 2 - dz, column] = 1
            for c in range(3):
                for yo in range(4):
                    for yi in range(6):
                        if 0 <= yo + 2 - yi < 3:
                            select_back[dx, yi, dz, c * 4 + yo, c, 2 - dx, yo + 2 - yi, dz] = 1
    select_in = select_in.reshape(81, 3 * PRE).astype(ml_dtypes.bfloat16)
    select_out = select_out.reshape(162, 3 * STR).astype(ml_dtypes.bfloat16)
    select_back = select_back.reshape(18 * 48, 81).astype(ml_dtypes.bfloat16)
    return dict(
        forward_z=forward_z,
        backward_z=backward_z,
        row_forward=row_forward,
        row_backward=row_backward,
        twiddle=twiddle,
        lane_forward=lane_forward,
        waves=waves,
        lane_backward=lane_backward,
        twiddle_back=twiddle_back,
        select_in=select_in,
        select_out=select_out,
        select_back=select_back,
    )


def split(value):
    high = value.astype(bf16)
    return high, (value - high.astype(f32)).astype(bf16)


def product(left, right, over=(1, 0)):
    dims = (((over[0],), (over[1],)), ((), ()))

    def one(a, b):
        return lax.dot_general(a, b, dims, preferred_element_type=f32)

    return one(left[0], right[0]) + (one(left[1], right[0]) + one(left[0], right[1]))


def fetch(pairs, sems):
    copies = [pltpu.make_async_copy(a, b, sems.at[i]) for i, (a, b) in enumerate(pairs)]
    for copy in copies:
        copy.start()
    return copies


def transform_z(source_far, table_far, out, source, table, sems):
    for copy in fetch([(source_far, source), (table_far, table)], sems):
        copy.wait()
    blocks = [[source[pl.ds(c * 64 + y, 16, stride=4), :] for y in range(4)] for c in range(3)]
    first = jnp.concatenate(blocks[0] + blocks[1], 0)
    second = jnp.concatenate(blocks[2] + blocks[2], 0)
    for tile, cells in enumerate((first, second)):
        modes = product((table[tile, 0], table[tile, 1]), split(cells), (1, 1))
        for copy in range(2):
            out[pl.ds(2 * copy + tile, 128, stride=4), :] = modes


def project(
    source_far,
    row_forward_far,
    twiddle_far,
    lane_forward_far,
    waves_far,
    lane_backward_far,
    twiddle_back_far,
    row_backward_far,
    out,
    source,
    row_forward,
    twiddle,
    lane_forward,
    waves,
    lane_backward,
    twiddle_back,
    row_backward,
    sems,
):
    device = lax.axis_index("px") * PY + lax.axis_index("py")
    part = lax.rem(device, 2)
    kz = lax.div(device, 4).astype(f32)
    first, *copies = fetch(
        [
            (source_far, source),
            (row_forward_far, row_forward),
            (twiddle_far, twiddle),
            (lane_forward_far, lane_forward),
            (waves_far, waves),
            (lane_backward_far.at[part], lane_backward),
            (twiddle_back_far.at[part], twiddle_back),
            (row_backward_far, row_backward),
        ],
        sems,
    )
    first.wait()
    copies[0].wait()
    tiles = [source[pl.ds(tile, 256, stride=2), :] for tile in range(2)]
    mixed = product((row_forward[0], row_forward[1]), split(jnp.concatenate(tiles, 1)))
    copies[1].wait()
    copies[2].wait()
    cos, sin = twiddle[0], twiddle[1]
    spectrum = []
    for tile in range(2):
        real = mixed[:256, tile * 128 : tile * 128 + 128]
        imag = mixed[256:, tile * 128 : tile * 128 + 128]
        turned = jnp.concatenate([real * cos - imag * sin, real * sin + imag * cos], 1)
        spectrum.append(product(split(turned), (lane_forward[0], lane_forward[1])))
    copies[3].wait()
    wave, square, retain = waves[0], waves[1], waves[2]
    inverse = 1.0 / jnp.maximum(square + kz * kz, 1.0)
    (hr, hi), (vr, vi) = [(s[:, :128], s[:, 128:]) for s in spectrum]
    flat_r, flat_i = hr * wave, hi * wave
    flat_r = flat_r + pltpu.roll(flat_r, 64, 1)
    flat_i = flat_i + pltpu.roll(flat_i, 64, 1)
    dot_r = (flat_r + kz * vi) * inverse
    dot_i = (flat_i - kz * vr) * inverse
    flat = jnp.concatenate([(hr - wave * dot_r) * retain, (hi - wave * dot_i) * retain], 1)
    upright = jnp.concatenate([(vr + kz * dot_i) * retain, (vi - kz * dot_r) * retain], 1)
    flat, upright = split(flat), split(upright)
    copies[4].wait()
    copies[5].wait()
    cos, sin = twiddle_back[0], twiddle_back[1]
    parts = []
    for component in range(3):
        matrix = lane_backward.at[component % 2]
        cells = product(upright if component == 2 else flat, (matrix[0], matrix[1]))
        real, imag = cells[:, :128], cells[:, 128:]
        parts.append(jnp.concatenate([real * cos - imag * sin, real * sin + imag * cos], 0))
    copies[6].wait()
    result = product((row_backward[0], row_backward[1]), split(jnp.concatenate(parts, 1)))
    for component in range(3):
        block = result[:, component * 128 : component * 128 + 128]
        out[pl.ds(component, 256, stride=3), :] = block


def extend_x(source, low, high, out):
    for c in range(3):
        for y in range(4):
            base = (c * 4 + y) * 24
            out[pl.ds(base + 16, 8), :] = jnp.zeros((8, 128), f32)
            out[pl.ds(base, 16), :] = source[pl.ds(c * 64 + y, 16, stride=4), :]
            out[pl.ds(base + 16, 3), :] = high[pl.ds(c * 12 + y, 3, stride=4), :]
            out[pl.ds(base + 21, 3), :] = low[pl.ds(c * 12 + y, 3, stride=4), :]


def sixth(at):
    near, middle, far = [at(k) - at(-k) for k in (1, 2, 3)]
    return (45.0 * near - 9.0 * middle + far) * (1.0 / (60.0 * spacing))


def rolled(block, axis):
    return lambda k: pltpu.roll(block, (-k) % block.shape[axis], axis)


def band_weights(
    kernel_in,
    kernel_out,
    select_in,
    select_out,
    select_back,
    banded_in,
    banded_out,
    banded_back,
):
    over_rows = (((0,), (0,)), ((), ()))
    for kernel, select, banded in (
        (kernel_in, select_in, banded_in),
        (kernel_out, select_out, banded_out),
    ):
        band = lax.dot_general(kernel[...], select[...], over_rows, preferred_element_type=f32)
        for yo in range(6):
            moved = band
            if yo:
                moved = jnp.concatenate([jnp.zeros((32, yo), f32), band[:, :-yo]], 1)
            banded[pl.ds(yo * 32, 32), :] = moved.astype(bf16)
    band = jnp.dot(select_back[...], kernel_in[...], preferred_element_type=f32).astype(bf16)
    for block in range(18):
        banded_back[:, pl.ds(block * 32, 32)] = band[block * 48 : block * 48 + 48]


def prepare(own, low, high, bias, banded_in, field, slope, slants, slabs, sems):
    pairs = []
    for c in range(3):
        for source, start, rows in ((low, 0, 72), (own, 72, 96), (high, 168, 72)):
            target = field.at[pl.ds(c * 240 + start, rows), :]
            pairs.append((source.at[pl.ds(c * rows, rows), :], target))
    for copy in fetch(pairs, sems):
        copy.wait()

    for i in range(20):
        row = (i + 22) % 24
        parts = [field[pl.ds(c * 240 + 24 + row, 8, stride=24), :] for c in range(3)]
        slab = jnp.concatenate(parts, 0)
        shifts = [pltpu.roll(slab, 1, 1), slab, pltpu.roll(slab, 127, 1)]
        slab = jnp.concatenate(shifts + [jnp.zeros((8, 128), f32)], 0).astype(bf16)
        for half, j in enumerate((i, i - 9)):
            if 0 <= j <= 10:
                slabs[pl.ds(j * PRE, PRE), pl.ds(half * 128, 128)] = slab
    for i in range(9):
        cells = slabs[pl.ds(i * PRE, 3 * PRE), :]
        value = jnp.dot(banded_in[...], cells, preferred_element_type=f32) + bias[...]
        value = jnp.tanh(value)
        slope[pl.ds(i * 192, 192), :] = 1.0 - value * value
    for a in range(3):
        for y in range(4):
            base = a * 240 + (y + 3) * 24
            block = field[pl.ds(base, 24), :]
            inner = block[:16]
            along = [
                sixth(rolled(block, 0))[:16],
                sixth(lambda k, base=base: field[pl.ds(base + 24 * k, 16), :]),
                sixth(rolled(inner, 1)),
            ]
            for c in range(3):
                slants[pl.ds(((a * 3 + c) * 4 + y) * 16, 16), :] = along[c]


def finish(
    modes_far,
    table_far,
    field_far,
    slants_far,
    slope_far,
    banded_out_far,
    banded_back_far,
    out,
    modes,
    table,
    field,
    slants,
    slope,
    banded_out,
    banded_back,
    lam,
    stress,
    slabs,
    adjoint,
    closure,
    sems,
):
    copies = fetch(
        [
            (modes_far, modes),
            (table_far, table),
            (banded_out_far, banded_out),
            (slope_far, slope),
            (banded_back_far, banded_back),
            (field_far, field),
            (slants_far, slants),
        ],
        sems,
    )
    copies[0].wait()
    copies[1].wait()
    for c in range(3):
        matrix = table.at[c // 2]
        for part in range(2):
            cells = split(modes[pl.ds(part * 3 + c, 128, stride=6), :])
            values = product(cells, (matrix[0], matrix[1]), (0, 0))
            lam[pl.ds(c * 240 + part * 120, 120), :] = values[:120]
    scale = 1.0 / (2.0 * spacing)
    for y in range(8):
        blocks = [lam[pl.ds(c * 240 + (y + 1) * 24, 24), :] for c in range(3)]
        along_x = [(pltpu.roll(b, 23, 0) - pltpu.roll(b, 1, 0)) * scale for b in blocks]
        along_z = [(pltpu.roll(b, 127, 1) - pltpu.roll(b, 1, 1)) * scale for b in blocks]
        along_y = [
            (lam[pl.ds(c * 240 + (y + 2) * 24, 24), :] - lam[pl.ds(c * 240 + y * 24, 24), :]) * scale
            for c in range(3)
        ]
        values = [
            along_x[0],
            along_y[1],
            along_z[2],
            along_y[0] + along_x[1],
            along_z[0] + along_x[2],
            along_z[1] + along_y[2],
        ]
        for s in range(6):
            stress[pl.ds((s * 8 + y) * 24, 24), :] = values[s]
    for i in range(20):
        slab = stress[pl.ds((i + 22) % 24, 48, stride=24), :]
        shifts = [pltpu.roll(slab, 1, 1), slab, pltpu.roll(slab, 127, 1)]
        slab = jnp.concatenate(shifts, 0).astype(bf16)
        for half, j in enumerate((i, i - 9)):
            if 0 <= j <= 10:
                slabs[pl.ds(j * STR, STR), pl.ds(half * 128, 128)] = slab
    copies[2].wait()
    copies[3].wait()
    for i in range(9):
        cells = slabs[pl.ds(i * STR, 3 * STR), :]
        value = jnp.dot(banded_out[...], cells, preferred_element_type=f32)
        value = (value * slope[pl.ds(i * 192, 192), :]).astype(bf16)
        for x, block in ((i, value[:, :128]), (i + 9, value[:, 128:])):
            for half, j in enumerate((x, x - 8)):
                if 0 <= j <= 9:
                    adjoint[pl.ds(j * 192, 192), pl.ds(half * 128, 128)] = block
    copies[4].wait()
    for i in range(8):
        cells = adjoint[pl.ds(i * 192, 576), :]
        value = jnp.dot(banded_back[...], cells, preferred_element_type=f32)
        for half in range(2):
            block = value[:, half * 128 : half * 128 + 128]
            total = block[16:32] + pltpu.roll(block[:16], 127, 1) + pltpu.roll(block[32:], 1, 1)
            closure[pl.ds((i + 8 * half) * 16, 16), :] = total
    copies[5].wait()
    copies[6].wait()
    for c in range(3):
        across = [
            lam[pl.ds(c * 240 + y * 24, 16), :] * field[pl.ds(240 + y * 24, 16), :]
            for y in range(10)
        ]
        for y in range(4):
            base = (y + 3) * 24
            block = lam[pl.ds(c * 240 + base, 24), :]
            total = sixth(rolled(block * field[pl.ds(base, 24), :], 0))[:16]
            total = total + sixth(lambda k, y=y: across[y + 3 + k])
            total = total + sixth(rolled(block[:16] * field[pl.ds(480 + base, 16), :], 1))
            crossed = [
                lam[pl.ds(a * 240 + base, 16), :] * slants[pl.ds(((a * 3 + c) * 4 + y) * 16, 16), :]
                for a in range(3)
            ]
            total = total - (crossed[0] + crossed[1] + crossed[2])
            total = total + closure[pl.ds(c * 4 + y, 16, stride=16), :]
            out[pl.ds(c * 64 + y, 16, stride=4), :] = block[:16] + time_step * total


def call(kernel, shapes, args, spaces, scratch=(), copies=0, limit=24 * 2**20, flops=0):
    size = 4 * sum(math.prod(s.shape) for s in shapes) + 4 * sum(math.prod(a.shape) for a in args)
    kinds = {"v": pltpu.VMEM, "s": pltpu.SMEM, "h": pltpu.HBM}
    scratch = list(scratch) + ([pltpu.SemaphoreType.DMA((copies,))] if copies else [])
    return pl.pallas_call(
        kernel,
        out_shape=shapes,
        in_specs=[pl.BlockSpec(memory_space=kinds[space]) for space in spaces],
        out_specs=[pl.BlockSpec(memory_space=pltpu.VMEM)] * len(shapes),
        scratch_shapes=scratch,
        compiler_params=pltpu.CompilerParams(vmem_limit_bytes=limit),
        cost_estimate=pl.CostEstimate(flops=flops, bytes_accessed=size, transcendentals=0),
    )(*args)


def shape(rows, columns=128, kind=f32):
    return jax.ShapeDtypeStruct((rows, columns), kind)


def body(velocity, cotangent, weight_in, bias_in, weight_out):
    t = {name: jnp.asarray(value) for name, value in constants().items()}
    (modes,) = call(
        transform_z,
        [shape(512)],
        [cotangent.reshape(192, 128), t["forward_z"]],
        "hh",
        [pltpu.VMEM((192, 128), f32), pltpu.VMEM((2, 2, 128, 128), bf16)],
        2,
        limit=FULL,
        flops=4 * 2**22,
    )
    modes, velocity, weight_in, bias_in, weight_out = lax.optimization_barrier(
        (modes, velocity, weight_in, bias_in, weight_out)
    )
    planes = lax.all_to_all(modes.reshape(256, 256), ("px", "py"), 0, 0, tiled=True)
    planes = planes.reshape(512, 128)

    up_x = [(i, (i + 1) % PX) for i in range(PX)]
    down_x = [(b, a) for a, b in up_x]
    up_y = [(i, (i + 1) % PY) for i in range(PY)]
    down_y = [(b, a) for a, b in up_y]
    low = lax.ppermute(velocity[:, 13:].reshape(36, 128), "px", up_x)
    high = lax.ppermute(velocity[:, :3].reshape(36, 128), "px", down_x)
    (own,) = call(extend_x, [shape(288)], [velocity.reshape(192, 128), low, high], "vvv")
    kernel_in = weight_in.reshape(32, 81).T
    kernel_out = weight_out.transpose(0, 2, 3, 4, 1).reshape(162, 32)
    banded_in, banded_out, banded_back = call(
        band_weights,
        [shape(192, 3 * PRE, bf16), shape(192, 3 * STR, bf16), shape(48, 576, bf16)],
        [kernel_in, kernel_out, t["select_in"], t["select_out"], t["select_back"]],
        "vvvvv",
        flops=2**27,
    )
    bias = jnp.tile(bias_in, 6).reshape(192, 1)
    planes, own, bias, banded_in, banded_out, banded_back = lax.optimization_barrier(
        (planes, own, bias, banded_in, banded_out, banded_back)
    )
    tables = [
        t["row_forward"],
        t["twiddle"],
        t["lane_forward"],
        t["waves"],
        t["lane_backward"],
        t["twiddle_back"],
        t["row_backward"],
    ]
    picked = {4: 1, 5: 1}
    (returned,) = call(
        project,
        [shape(768)],
        [planes] + tables,
        "h" * 8,
        [pltpu.VMEM((512, 128), f32)]
        + [pltpu.VMEM(a.shape[picked.get(i, 0) :], a.dtype) for i, a in enumerate(tables)],
        8,
        limit=MOST,
        flops=30 * 2 * 256**3,
    )
    received = lax.all_to_all(returned.reshape(256, 384), ("px", "py"), 0, 0, tiled=True)
    layers = own.reshape(3, 96, 128)
    low = lax.ppermute(layers[:, 24:].reshape(216, 128), "py", up_y)
    high = lax.ppermute(layers[:, :72].reshape(216, 128), "py", down_y)
    field, slope, slants = call(
        prepare,
        [shape(720), shape(9 * 192, 256), shape(576)],
        [own, low, high, bias, banded_in],
        "hhhvv",
        [pltpu.VMEM((11 * PRE, 256), bf16)],
        9,
        limit=FULL,
        flops=18 * 2 * 192 * 256 * 128,
    )
    operands = [
        received.reshape(768, 128),
        t["backward_z"],
        field,
        slants,
        slope,
        banded_out,
        banded_back,
    ]
    (result,) = call(
        finish,
        [shape(192)],
        operands,
        "h" * 7,
        [pltpu.VMEM(a.shape, a.dtype) for a in operands]
        + [
            pltpu.VMEM((720, 128), f32),
            pltpu.VMEM((48 * 24, 128), f32),
            pltpu.VMEM((11 * STR, 256), bf16),
            pltpu.VMEM((10 * 192, 256), bf16),
            pltpu.VMEM((256, 128), f32),
        ],
        7,
        limit=MOST,
        flops=2**29,
    )
    return result.reshape(3, 16, 4, 128)


def solution(mesh):
    placed = (P(None, "px", "py", None), P(None, "px", "py", None), P(), P(), P())
    return jax.shard_map(
        body, mesh=mesh, in_specs=placed, out_specs=P(None, "px", "py", None), check_vma=False
    )
```

```python
import functools
import math

import jax
import jax.numpy as jnp
import ml_dtypes
import numpy as np
from jax import lax
from jax.experimental import pallas as pl
from jax.experimental.pallas import tpu as pltpu
from jax.sharding import PartitionSpec as P

N = 128
PX = 8
PY = 32
time_step = 0.005
spacing = 2.0 * math.pi / N
bf16 = jnp.bfloat16
f32 = jnp.float32
MOST = 2**26 - 2**14
PRE = 80
STR = 144


def halves(table):
    table = np.asarray(table, np.float64)
    high = table.astype(np.float32).astype(ml_dtypes.bfloat16)
    low = (table - high.astype(np.float64)).astype(np.float32).astype(ml_dtypes.bfloat16)
    return np.stack([high, low])


def complex_form(table):
    return np.block([[table.real, table.imag], [-table.imag, table.real]])


@functools.cache
def constants():
    z = np.arange(N)
    kz = np.arange(N // 2)
    angle = 2 * np.pi * ((kz[:, None] * z[None]) % N) / N
    cos, sin = np.cos(angle), np.sin(angle)
    weight = np.where(kz == 0, 1.0, 2.0)[:, None] / float(N) ** 3

    def pair(first, second):
        return np.stack([first, second], 1).reshape(N, N)

    forward_z = np.stack([halves(pair(cos, -sin)), halves(pair(sin, cos))])
    backward_z = np.stack(
        [halves(pair(cos * weight, -sin * weight)), halves(pair(sin * weight, cos * weight))]
    )
    a, b = np.arange(PX), np.arange(PY)
    y4, x16 = np.arange(4), np.arange(16)
    phase = a[:, None, None, None] * a[None, None, :, None] / PX
    phase = phase + b[None, :, None, None] * b[None, None, None, :] / PY
    rows = np.exp(-2j * np.pi * phase.reshape(256, 256))
    row_forward = halves(np.concatenate([rows.real, rows.imag], 0))
    row_backward = halves(np.concatenate([rows.real, rows.imag], 1))
    phase = a[:, None, None, None] * x16 + b[None, :, None, None] * y4[:, None]
    twiddle = np.exp(-2j * np.pi * phase.reshape(256, 64) / N)
    twiddle = np.tile(twiddle, (1, 2))
    twiddle = np.stack([twiddle.real, twiddle.imag]).astype(np.float32)
    phase = y4[:, None, None, None] * y4[:, None] / 4 + x16[:, None, None] * x16 / 16
    lanes = np.exp(-2j * np.pi * phase.reshape(64, 64))
    lane_forward = halves(complex_form(np.kron(np.eye(2), lanes)))
    m, l = np.broadcast_arrays(
        a[:, None, None, None] + 8 * x16, b[None, :, None, None] + 32 * y4[:, None]
    )
    m, l = m.reshape(256, 64), l.reshape(256, 64)
    kx, ky = np.where(m > 64, m - N, m), np.where(l > 64, l - N, l)
    square = np.tile(kx * kx + ky * ky, (1, 2))
    retain = np.tile((m != 64) & (l != 64), (1, 2))
    waves = np.stack([np.concatenate([kx, ky], 1), square, retain]).astype(np.float32)
    r = np.arange(24)
    xe = np.where(r < 19, r, r - 24)
    lane_backward, twiddle_back = [], []
    for part in range(2):
        ye = np.arange(5) + (5 * part - 3)
        phase = y4[:, None, None, None] * ye[:, None] / 4 + x16[:, None, None] * xe / 16
        table = np.pad(np.exp(2j * np.pi * phase.reshape(64, 120)), ((0, 0), (0, 8)))
        for component in range(2):
            pick = np.eye(2)[:, component : component + 1]
            lane_backward.append(halves(complex_form(np.kron(pick, table))))
        phase = a[:, None, None, None] * xe + b[None, :, None, None] * ye[:, None]
        table = np.pad(np.exp(2j * np.pi * phase.reshape(256, 120) / N), ((0, 0), (0, 8)))
        twiddle_back.append(np.stack([table.real, table.imag]))
    lane_backward = np.stack(lane_backward).reshape(2, 2, 2, 256, 256)
    twiddle_back = np.stack(twiddle_back).astype(np.float32)
    select_in = np.zeros((3, 3, 3, 3, 3 * PRE))
    select_out = np.zeros((6, 3, 3, 3, 3 * STR))
    select_back = np.zeros((3, 6, 3, 16, 3, 3, 3, 3))
    for dx in range(3):
        for dz in range(3):
            for dy in range(3):
                for c in range(3):
                    select_in[c, dx, dy, dz, dx * PRE + dz * 24 + c * 8 + dy] = 1
                for s in range(6):
                    column = dx * STR + dz * 48 + s * 8 + dy
                    select_out[s, 2 - dx, 2 - dy, 2 - dz, column] = 1
            for c in range(3):
                for yo in range(4):
                    for yi in range(6):
                        if 0 <= yo + 2 - yi < 3:
                            select_back[dx, yi, dz, c * 4 + yo, c, 2 - dx, yo + 2 - yi, dz] = 1
    select_in = select_in.reshape(81, 3 * PRE).astype(ml_dtypes.bfloat16)
    select_out = select_out.reshape(162, 3 * STR).astype(ml_dtypes.bfloat16)
    select_back = select_back.reshape(18 * 48, 81).astype(ml_dtypes.bfloat16)
    return dict(
        forward_z=forward_z,
        backward_z=backward_z,
        row_forward=row_forward,
        row_backward=row_backward,
        twiddle=twiddle,
        lane_forward=lane_forward,
        waves=waves,
        lane_backward=lane_backward,
        twiddle_back=twiddle_back,
        select_in=select_in,
        select_out=select_out,
        select_back=select_back,
    )


def split(value):
    high = value.astype(bf16)
    return high, (value - high.astype(f32)).astype(bf16)


def product(left, right, over=(1, 0)):
    dims = (((over[0],), (over[1],)), ((), ()))

    def one(a, b):
        return lax.dot_general(a, b, dims, preferred_element_type=f32)

    return one(left[0], right[0]) + (one(left[1], right[0]) + one(left[0], right[1]))


def fetch(pairs, sems, at=0):
    copies = [pltpu.make_async_copy(a, b, sems.at[at + i]) for i, (a, b) in enumerate(pairs)]
    for copy in copies:
        copy.start()
    return copies


def transform_z(source_far, table_far, velocity, out, last, first, source, table, sems):
    pairs = [(source_far, source), (table_far, table)]
    for c in range(3):
        rows = pl.ds(c * 12, 12)
        pairs.append((velocity.at[pl.ds(c * 64 + 52, 12), :], last.at[rows, :]))
        pairs.append((velocity.at[pl.ds(c * 64, 12), :], first.at[rows, :]))
    copies = fetch(pairs, sems)
    copies[0].wait()
    copies[1].wait()
    blocks = [[source[pl.ds(c * 64 + y, 16, stride=4), :] for y in range(4)] for c in range(3)]
    flat = jnp.concatenate(blocks[0] + blocks[1], 0)
    upright = jnp.concatenate(blocks[2] + blocks[2], 0)
    for tile, cells in enumerate((flat, upright)):
        modes = product((table[tile, 0], table[tile, 1]), split(cells), (1, 1))
        for copy in range(2):
            out[pl.ds(2 * copy + tile, 128, stride=4), :] = modes
    for copy in copies[2:]:
        copy.wait()


def project(
    source_far,
    row_forward_far,
    twiddle_far,
    lane_forward_far,
    waves_far,
    lane_backward_far,
    twiddle_back_far,
    row_backward_far,
    out,
    source,
    row_forward,
    twiddle,
    lane_forward,
    waves,
    lane_backward,
    twiddle_back,
    row_backward,
    sems,
):
    device = lax.axis_index("px") * PY + lax.axis_index("py")
    part = lax.rem(device, 2)
    kz = lax.div(device, 4).astype(f32)
    first, *copies = fetch(
        [
            (source_far, source),
            (row_forward_far, row_forward),
            (twiddle_far, twiddle),
            (lane_forward_far, lane_forward),
        ],
        sems,
    )
    first.wait()
    copies[0].wait()
    copies += fetch(
        [
            (waves_far, waves),
            (lane_backward_far.at[part], lane_backward),
            (twiddle_back_far.at[part], twiddle_back),
            (row_backward_far, row_backward),
        ],
        sems,
        4,
    )
    tiles = [source[pl.ds(tile, 256, stride=2), :] for tile in range(2)]
    mixed = product((row_forward[0], row_forward[1]), split(jnp.concatenate(tiles, 1)))
    copies[1].wait()
    copies[2].wait()
    cos, sin = twiddle[0], twiddle[1]
    spectrum = []
    for tile in range(2):
        real = mixed[:256, tile * 128 : tile * 128 + 128]
        imag = mixed[256:, tile * 128 : tile * 128 + 128]
        turned = jnp.concatenate([real * cos - imag * sin, real * sin + imag * cos], 1)
        spectrum.append(product(split(turned), (lane_forward[0], lane_forward[1])))
    copies[3].wait()
    wave, square, retain = waves[0], waves[1], waves[2]
    inverse = 1.0 / jnp.maximum(square + kz * kz, 1.0)
    (hr, hi), (vr, vi) = [(s[:, :128], s[:, 128:]) for s in spectrum]
    flat_r, flat_i = hr * wave, hi * wave
    flat_r = flat_r + pltpu.roll(flat_r, 64, 1)
    flat_i = flat_i + pltpu.roll(flat_i, 64, 1)
    dot_r = (flat_r + kz * vi) * inverse
    dot_i = (flat_i - kz * vr) * inverse
    flat = jnp.concatenate([(hr - wave * dot_r) * retain, (hi - wave * dot_i) * retain], 1)
    upright = jnp.concatenate([(vr + kz * dot_i) * retain, (vi - kz * dot_r) * retain], 1)
    flat, upright = split(flat), split(upright)
    copies[4].wait()
    copies[5].wait()
    cos, sin = twiddle_back[0], twiddle_back[1]
    parts = []
    for component in range(3):
        matrix = lane_backward.at[component % 2]
        cells = product(upright if component == 2 else flat, (matrix[0], matrix[1]))
        real, imag = cells[:, :128], cells[:, 128:]
        parts.append(jnp.concatenate([real * cos - imag * sin, real * sin + imag * cos], 0))
    copies[6].wait()
    result = product((row_backward[0], row_backward[1]), split(jnp.concatenate(parts, 1)))
    for component in range(3):
        block = result[:, component * 128 : component * 128 + 128]
        out[pl.ds(component, 256, stride=3), :] = block


def arrange(
    velocity_far,
    low_far,
    high_far,
    kernel_in_far,
    kernel_out_far,
    bias_far,
    select_in_far,
    select_out_far,
    select_back_far,
    own,
    last,
    first,
    bias_rows,
    banded_in,
    banded_out,
    banded_back,
    velocity,
    low,
    high,
    kernel_in,
    kernel_out,
    bias,
    select_in,
    select_out,
    select_back,
    lines_in,
    lines_out,
    sems,
):
    far = [velocity_far, low_far, high_far, kernel_in_far, kernel_out_far, bias_far]
    far += [select_in_far, select_out_far, select_back_far]
    near = [velocity, low, high, kernel_in, kernel_out, bias, select_in, select_out, select_back]
    for copy in fetch(list(zip(far, near)), sems):
        copy.wait()
    for c in range(3):
        for y in range(4):
            targets = [(own, (c * 4 + y) * 24)]
            if y > 0:
                targets.append((last, (c * 3 + y - 1) * 24))
            if y < 3:
                targets.append((first, (c * 3 + y) * 24))
            for out, base in targets:
                out[pl.ds(base + 16, 8), :] = jnp.zeros((8, 128), f32)
                out[pl.ds(base, 16), :] = velocity[pl.ds(c * 64 + y, 16, stride=4), :]
                out[pl.ds(base + 16, 3), :] = high[pl.ds(c * 12 + y, 3, stride=4), :]
                out[pl.ds(base + 21, 3), :] = low[pl.ds(c * 12 + y, 3, stride=4), :]
    square = (32, 32)
    diagonal = lax.broadcasted_iota(jnp.int32, square, 0) == lax.broadcasted_iota(
        jnp.int32, square, 1
    )
    column = jnp.sum(jnp.where(diagonal, jnp.broadcast_to(bias[...], square), 0.0), 1, keepdims=True)
    column = jnp.broadcast_to(column, (32, 128))
    for yo in range(6):
        bias_rows[pl.ds(yo * 32, 32), :] = column
    for kernel, lines, count in ((kernel_in, lines_in, 3), (kernel_out, lines_out, 6)):
        for c in range(count):
            for dx in range(3):
                for dy in range(3):
                    rows = pl.ds(((c * 3 + dx) * 3 + dy) * 3, 3)
                    lines[rows, :] = kernel[c, dx, dy].astype(f32)
    lines = lines_in[...].astype(bf16)
    over_rows = (((0,), (0,)), ((), ()))
    for kernel, select, banded in (
        (lines, select_in, banded_in),
        (lines_out[...].astype(bf16), select_out, banded_out),
    ):
        band = lax.dot_general(kernel, select[...], over_rows, preferred_element_type=f32)
        for yo in range(6):
            moved = band
            if yo:
                moved = jnp.concatenate([jnp.zeros((32, yo), f32), band[:, :-yo]], 1)
            banded[pl.ds(yo * 32, 32), :] = moved.astype(bf16)
    band = jnp.dot(select_back[...], lines, preferred_element_type=f32).astype(bf16)
    for block in range(18):
        banded_back[:, pl.ds(block * 32, 32)] = band[block * 48 : block * 48 + 48]


def sixth(at):
    near, middle, far = [at(k) - at(-k) for k in (1, 2, 3)]
    return (45.0 * near - 9.0 * middle + far) * (1.0 / (60.0 * spacing))


def rolled(block, axis):
    return lambda k: pltpu.roll(block, (-k) % block.shape[axis], axis)


def prepare(
    own,
    low,
    high,
    bias_far,
    banded_in_far,
    field,
    slope,
    slants,
    slabs,
    bias,
    banded_in,
    sems,
):
    pairs = [(bias_far, bias), (banded_in_far, banded_in)]
    for c in range(3):
        for source, start, rows in ((low, 0, 72), (own, 72, 96), (high, 168, 72)):
            target = field.at[pl.ds(c * 240 + start, rows), :]
            pairs.append((source.at[pl.ds(c * rows, rows), :], target))
    for copy in fetch(pairs, sems):
        copy.wait()

    lift = jnp.concatenate([bias[...], bias[...]], 1)
    for i in range(20):
        row = (i + 22) % 24
        parts = [field[pl.ds(c * 240 + 24 + row, 8, stride=24), :] for c in range(3)]
        slab = jnp.concatenate(parts, 0)
        shifts = [pltpu.roll(slab, 1, 1), slab, pltpu.roll(slab, 127, 1)]
        slab = jnp.concatenate(shifts + [jnp.zeros((8, 128), f32)], 0).astype(bf16)
        for half, j in enumerate((i, i - 9)):
            if 0 <= j <= 10:
                slabs[pl.ds(j * PRE, PRE), pl.ds(half * 128, 128)] = slab
    for i in range(9):
        cells = slabs[pl.ds(i * PRE, 3 * PRE), :]
        value = jnp.dot(banded_in[...], cells, preferred_element_type=f32) + lift
        value = jnp.tanh(value)
        slope[pl.ds(i * 192, 192), :] = 1.0 - value * value
    for a in range(3):
        for y in range(4):
            base = a * 240 + (y + 3) * 24
            block = field[pl.ds(base, 24), :]
            inner = block[:16]
            along = [
                sixth(rolled(block, 0))[:16],
                sixth(lambda k, base=base: field[pl.ds(base + 24 * k, 16), :]),
                sixth(rolled(inner, 1)),
            ]
            for c in range(3):
                slants[pl.ds(((a * 3 + c) * 4 + y) * 16, 16), :] = along[c]


def finish(
    modes_far,
    table_far,
    field_far,
    slants_far,
    slope_far,
    banded_out_far,
    banded_back_far,
    out,
    modes,
    table,
    field,
    slants,
    slope,
    banded_out,
    banded_back,
    lam,
    stress,
    slabs,
    adjoint,
    closure,
    sems,
):
    copies = fetch(
        [
            (modes_far, modes),
            (table_far, table),
            (banded_out_far, banded_out),
            (slope_far, slope),
            (banded_back_far, banded_back),
            (field_far, field),
            (slants_far, slants),
        ],
        sems,
    )
    copies[0].wait()
    copies[1].wait()
    for c in range(3):
        matrix = table.at[c // 2]
        for part in range(2):
            cells = split(modes[pl.ds(part * 3 + c, 128, stride=6), :])
            values = product(cells, (matrix[0], matrix[1]), (0, 0))
            lam[pl.ds(c * 240 + part * 120, 120), :] = values[:120]
    scale = 1.0 / (2.0 * spacing)
    for y in range(8):
        blocks = [lam[pl.ds(c * 240 + (y + 1) * 24, 24), :] for c in range(3)]
        along_x = [(pltpu.roll(b, 23, 0) - pltpu.roll(b, 1, 0)) * scale for b in blocks]
        along_z = [(pltpu.roll(b, 127, 1) - pltpu.roll(b, 1, 1)) * scale for b in blocks]
        along_y = [
            (lam[pl.ds(c * 240 + (y + 2) * 24, 24), :] - lam[pl.ds(c * 240 + y * 24, 24), :]) * scale
            for c in range(3)
        ]
        values = [
            along_x[0],
            along_y[1],
            along_z[2],
            along_y[0] + along_x[1],
            along_z[0] + along_x[2],
            along_z[1] + along_y[2],
        ]
        for s in range(6):
            stress[pl.ds((s * 8 + y) * 24, 24), :] = values[s]
    for i in range(20):
        slab = stress[pl.ds((i + 22) % 24, 48, stride=24), :]
        shifts = [pltpu.roll(slab, 1, 1), slab, pltpu.roll(slab, 127, 1)]
        slab = jnp.concatenate(shifts, 0).astype(bf16)
        for half, j in enumerate((i, i - 9)):
            if 0 <= j <= 10:
                slabs[pl.ds(j * STR, STR), pl.ds(half * 128, 128)] = slab
    copies[2].wait()
    copies[3].wait()
    for i in range(9):
        cells = slabs[pl.ds(i * STR, 3 * STR), :]
        value = jnp.dot(banded_out[...], cells, preferred_element_type=f32)
        value = (value * slope[pl.ds(i * 192, 192), :]).astype(bf16)
        for x, block in ((i, value[:, :128]), (i + 9, value[:, 128:])):
            for half, j in enumerate((x, x - 8)):
                if 0 <= j <= 9:
                    adjoint[pl.ds(j * 192, 192), pl.ds(half * 128, 128)] = block
    copies[4].wait()
    for i in range(8):
        cells = adjoint[pl.ds(i * 192, 576), :]
        value = jnp.dot(banded_back[...], cells, preferred_element_type=f32)
        for half in range(2):
            block = value[:, half * 128 : half * 128 + 128]
            total = block[16:32] + pltpu.roll(block[:16], 127, 1) + pltpu.roll(block[32:], 1, 1)
            closure[pl.ds((i + 8 * half) * 16, 16), :] = total
    copies[5].wait()
    copies[6].wait()
    for c in range(3):
        across = [
            lam[pl.ds(c * 240 + y * 24, 16), :] * field[pl.ds(240 + y * 24, 16), :]
            for y in range(10)
        ]
        for y in range(4):
            base = (y + 3) * 24
            block = lam[pl.ds(c * 240 + base, 24), :]
            total = sixth(rolled(block * field[pl.ds(base, 24), :], 0))[:16]
            total = total + sixth(lambda k, y=y: across[y + 3 + k])
            total = total + sixth(rolled(block[:16] * field[pl.ds(480 + base, 16), :], 1))
            crossed = [
                lam[pl.ds(a * 240 + base, 16), :] * slants[pl.ds(((a * 3 + c) * 4 + y) * 16, 16), :]
                for a in range(3)
            ]
            total = total - (crossed[0] + crossed[1] + crossed[2])
            total = total + closure[pl.ds(c * 4 + y, 16, stride=16), :]
            out[pl.ds(c * 64 + y, 16, stride=4), :] = block[:16] + time_step * total


def call(kernel, shapes, args, spaces, outs, scratch=(), copies=0, limit=MOST, flops=0):
    size = 4 * sum(math.prod(s.shape) for s in shapes) + 4 * sum(math.prod(a.shape) for a in args)
    kinds = {"v": pltpu.VMEM, "s": pltpu.SMEM, "h": pltpu.HBM}
    scratch = list(scratch) + ([pltpu.SemaphoreType.DMA((copies,))] if copies else [])
    return pl.pallas_call(
        kernel,
        out_shape=shapes,
        in_specs=[pl.BlockSpec(memory_space=kinds[space]) for space in spaces],
        out_specs=[pl.BlockSpec(memory_space=kinds[space]) for space in outs],
        scratch_shapes=scratch,
        compiler_params=pltpu.CompilerParams(vmem_limit_bytes=limit),
        cost_estimate=pl.CostEstimate(flops=flops, bytes_accessed=size, transcendentals=0),
    )(*args)


def shape(rows, columns=128, kind=f32):
    return jax.ShapeDtypeStruct((rows, columns), kind)


def body(velocity, cotangent, weight_in, bias_in, weight_out):
    t = {name: jnp.asarray(value) for name, value in constants().items()}
    modes, last, first = call(
        transform_z,
        [shape(512), shape(36), shape(36)],
        [cotangent.reshape(192, 128), t["forward_z"], velocity.reshape(192, 128)],
        "hhh",
        "vvv",
        [pltpu.VMEM((192, 128), f32), pltpu.VMEM((2, 2, 128, 128), bf16)],
        8,
        flops=4 * 2**22,
    )
    planes = lax.all_to_all(modes.reshape(256, 256), ("px", "py"), 0, 0, tiled=True)
    planes = planes.reshape(512, 128)

    up_x = [(i, (i + 1) % PX) for i in range(PX)]
    down_x = [(b, a) for a, b in up_x]
    up_y = [(i, (i + 1) % PY) for i in range(PY)]
    down_y = [(b, a) for a, b in up_y]
    low = lax.ppermute(last, "px", up_x)
    high = lax.ppermute(first, "px", down_x)
    planes, low, high = lax.optimization_barrier((planes, low, high))
    operands = [
        velocity.reshape(192, 128),
        low,
        high,
        weight_in.transpose(1, 2, 3, 4, 0),
        weight_out.transpose(0, 2, 3, 4, 1),
        bias_in.reshape(1, 32),
        t["select_in"],
        t["select_out"],
        t["select_back"],
    ]
    own, last, first, bias, banded_in, banded_out, banded_back = call(
        arrange,
        [shape(288), shape(216), shape(216), shape(192)]
        + [shape(192, 3 * PRE, bf16), shape(192, 3 * STR, bf16), shape(48, 576, bf16)],
        operands,
        "h" * 9,
        "v" * 7,
        [pltpu.VMEM(a.shape, a.dtype) for a in operands]
        + [pltpu.VMEM((81, 32), f32), pltpu.VMEM((162, 32), f32)],
        9,
        flops=2**27,
    )
    tables = [
        t["row_forward"],
        t["twiddle"],
        t["lane_forward"],
        t["waves"],
        t["lane_backward"],
        t["twiddle_back"],
        t["row_backward"],
    ]
    picked = {4: 1, 5: 1}
    (returned,) = call(
        project,
        [shape(768)],
        [planes] + tables,
        "h" * 8,
        "v",
        [pltpu.VMEM((512, 128), f32)]
        + [pltpu.VMEM(a.shape[picked.get(i, 0) :], a.dtype) for i, a in enumerate(tables)],
        8,
        flops=30 * 2 * 256**3,
    )
    received = lax.all_to_all(returned.reshape(256, 384), ("px", "py"), 0, 0, tiled=True)
    low = lax.ppermute(last, "py", up_y)
    high = lax.ppermute(first, "py", down_y)
    field, slope, slants = call(
        prepare,
        [shape(720), shape(9 * 192, 256), shape(576)],
        [own, low, high, bias, banded_in],
        "h" * 5,
        "vvv",
        [
            pltpu.VMEM((11 * PRE, 256), bf16),
            pltpu.VMEM((192, 128), f32),
            pltpu.VMEM((192, 3 * PRE), bf16),
        ],
        11,
        flops=18 * 2 * 192 * 256 * 128,
    )
    operands = [
        received.reshape(768, 128),
        t["backward_z"],
        field,
        slants,
        slope,
        banded_out,
        banded_back,
    ]
    (result,) = call(
        finish,
        [shape(192)],
        operands,
        "h" * 7,
        "v",
        [pltpu.VMEM(a.shape, a.dtype) for a in operands]
        + [
            pltpu.VMEM((720, 128), f32),
            pltpu.VMEM((48 * 24, 128), f32),
            pltpu.VMEM((11 * STR, 256), bf16),
            pltpu.VMEM((10 * 192, 256), bf16),
            pltpu.VMEM((256, 128), f32),
        ],
        7,
        flops=2**29,
    )
    return result.reshape(3, 16, 4, 128)


def solution(mesh):
    placed = (P(None, "px", "py", None), P(None, "px", "py", None), P(), P(), P())
    return jax.shard_map(
        body, mesh=mesh, in_specs=placed, out_specs=P(None, "px", "py", None), check_vma=False
    )
```

```python
import functools
import math

import jax
import jax.numpy as jnp
import ml_dtypes
import numpy as np
from jax import lax
from jax.experimental import pallas as pl
from jax.experimental.pallas import tpu as pltpu
from jax.sharding import PartitionSpec as P

N = 128
PX = 8
PY = 32
time_step = 0.005
spacing = 2.0 * math.pi / N
bf16 = jnp.bfloat16
f32 = jnp.float32
MOST = 2**26 - 2**14
PRE = 80
STR = 144


def halves(table):
    table = np.asarray(table, np.float64)
    high = table.astype(np.float32).astype(ml_dtypes.bfloat16)
    low = (table - high.astype(np.float64)).astype(np.float32).astype(ml_dtypes.bfloat16)
    return np.stack([high, low])


def complex_form(table):
    return np.concatenate([table.real, table.imag], 1)


@functools.cache
def constants():
    z = np.arange(N)
    kz = np.arange(N // 2)
    angle = 2 * np.pi * ((kz[:, None] * z[None]) % N) / N
    cos, sin = np.cos(angle), np.sin(angle)
    weight = np.where(kz == 0, 1.0, 2.0)[:, None] / float(N) ** 3

    def pair(first, second):
        return np.stack([first, second], 1).reshape(N, N)

    forward_z = np.stack([halves(pair(cos, -sin)), halves(pair(sin, cos))])
    backward_z = np.stack(
        [halves(pair(cos * weight, -sin * weight)), halves(pair(sin * weight, cos * weight))]
    )
    a, b = np.arange(PX), np.arange(PY)
    y4, x16 = np.arange(4), np.arange(16)
    phase = a[:, None, None, None] * a[None, None, :, None] / PX
    phase = phase + b[None, :, None, None] * b[None, None, None, :] / PY
    rows = np.exp(-2j * np.pi * phase.reshape(256, 256))
    row_forward = halves(np.concatenate([rows.real, rows.imag], 0))
    phase = a[:, None, None, None] * x16 + b[None, :, None, None] * y4[:, None]
    twiddle = np.exp(-2j * np.pi * phase.reshape(256, 64) / N)
    twiddle = np.tile(twiddle, (1, 2))
    twiddle = np.stack([twiddle.real, twiddle.imag]).astype(np.float32)
    phase = y4[:, None, None, None] * y4[:, None] / 4 + x16[:, None, None] * x16 / 16
    lanes = np.exp(-2j * np.pi * phase.reshape(64, 64))
    lane_forward = halves(complex_form(np.kron(np.eye(2), lanes)))
    m, l = np.broadcast_arrays(
        a[:, None, None, None] + 8 * x16, b[None, :, None, None] + 32 * y4[:, None]
    )
    m, l = m.reshape(256, 64), l.reshape(256, 64)
    kx, ky = np.where(m > 64, m - N, m), np.where(l > 64, l - N, l)
    waves = np.concatenate([kx, ky], 1).astype(np.float32)
    r = np.arange(24)
    xe = np.where(r < 19, r, r - 24)
    lane_backward, twiddle_back = [], []
    for part in range(2):
        ye = np.arange(5) + (5 * part - 3)
        phase = y4[:, None, None, None] * ye[:, None] / 4 + x16[:, None, None] * xe / 16
        table = np.pad(np.exp(2j * np.pi * phase.reshape(64, 120)), ((0, 0), (0, 8)))
        for component in range(2):
            pick = np.eye(2)[:, component : component + 1]
            lane_backward.append(halves(complex_form(np.kron(pick, table))))
        phase = a[:, None, None, None] * xe + b[None, :, None, None] * ye[:, None]
        table = np.pad(np.exp(2j * np.pi * phase.reshape(256, 120) / N), ((0, 0), (0, 8)))
        twiddle_back.append(np.stack([table.real, table.imag]))
    lane_backward = np.stack(lane_backward).reshape(2, 2, 2, 128, 256)
    twiddle_back = np.stack(twiddle_back).astype(np.float32)
    select_in = np.zeros((3, 3, 3, 3, 3 * PRE))
    select_out = np.zeros((6, 3, 3, 3, 3 * STR))
    select_back = np.zeros((3, 6, 3, 16, 3, 3, 3, 3))
    for dx in range(3):
        for dz in range(3):
            for dy in range(3):
                for c in range(3):
                    select_in[c, dx, dy, dz, dx * PRE + dz * 24 + c * 8 + dy] = 1
                for s in range(6):
                    column = dx * STR + dz * 48 + s * 8 + dy
                    select_out[s, 2 - dx, 2 - dy, 2 - dz, column] = 1
            for c in range(3):
                for yo in range(4):
                    for yi in range(6):
                        if 0 <= yo + 2 - yi < 3:
                            select_back[dx, yi, dz, c * 4 + yo, c, 2 - dx, yo + 2 - yi, dz] = 1
    select_in = select_in.reshape(81, 3 * PRE).astype(ml_dtypes.bfloat16)
    select_out = select_out.reshape(162, 3 * STR).astype(ml_dtypes.bfloat16)
    select_back = select_back.reshape(18 * 48, 81).astype(ml_dtypes.bfloat16)
    return dict(
        forward_z=forward_z,
        backward_z=backward_z,
        row_forward=row_forward,
        twiddle=twiddle,
        lane_forward=lane_forward,
        waves=waves,
        lane_backward=lane_backward,
        twiddle_back=twiddle_back,
        select_in=select_in,
        select_out=select_out,
        select_back=select_back,
    )


def split(value):
    high = value.astype(bf16)
    return high, (value - high.astype(f32)).astype(bf16)


def product(left, right, over=(1, 0)):
    left = jnp.concatenate([left[0], left[1], left[0]], over[0])
    right = jnp.concatenate([right[0], right[0], right[1]], over[1])
    dims = (((over[0],), (over[1],)), ((), ()))
    return lax.dot_general(left, right, dims, preferred_element_type=f32)


def turner(tables):
    whole = []
    for half in range(2):
        top = tables[half]
        bottom = jnp.concatenate([-top[:, 128:], top[:, :128]], 1)
        whole.append(jnp.concatenate([top, bottom], 0))
    return whole


def fetch(pairs, sems, at=0):
    copies = [pltpu.make_async_copy(a, b, sems.at[at + i]) for i, (a, b) in enumerate(pairs)]
    for copy in copies:
        copy.start()
    return copies


def transform_z(source_far, table_far, velocity, out, even, odd, source, table, sems):
    parity = lax.rem(lax.axis_index("px"), 2)
    copies = fetch(
        [
            (source_far, source),
            (table_far, table),
            (velocity.at[:, pl.ds(13 * (1 - parity), 3)], even),
            (velocity.at[:, pl.ds(13 * parity, 3)], odd),
        ],
        sems,
    )
    copies[0].wait()
    copies[1].wait()
    blocks = [[source[pl.ds(c * 64 + y, 16, stride=4), :] for y in range(4)] for c in range(3)]
    flat = jnp.concatenate(blocks[0] + blocks[1], 0)
    upright = jnp.concatenate(blocks[2] + blocks[2], 0)
    for tile, cells in enumerate((flat, upright)):
        modes = product((table[tile, 0], table[tile, 1]), split(cells), (1, 1))
        for copy in range(2):
            out[pl.ds(2 * copy + tile, 128, stride=4), :] = modes
    for copy in copies[2:]:
        copy.wait()


def project(
    source_far,
    row_forward_far,
    twiddle_far,
    lane_forward_far,
    waves_far,
    lane_backward_far,
    twiddle_back_far,
    out,
    source,
    row_forward,
    twiddle,
    lane_forward,
    waves,
    lane_backward,
    twiddle_back,
    sems,
):
    device = lax.axis_index("px") * PY + lax.axis_index("py")
    part = lax.rem(device, 2)
    kz = lax.div(device, 4).astype(f32)
    first, *copies = fetch(
        [
            (source_far, source),
            (row_forward_far, row_forward),
            (twiddle_far, twiddle),
            (lane_forward_far, lane_forward),
            (waves_far, waves),
            (lane_backward_far.at[part], lane_backward),
            (twiddle_back_far.at[part], twiddle_back),
        ],
        sems,
    )
    first.wait()
    copies[0].wait()
    tiles = [source[pl.ds(tile, 256, stride=2), :] for tile in range(2)]
    mixed = product((row_forward[0], row_forward[1]), split(jnp.concatenate(tiles, 1)))
    copies[1].wait()
    copies[2].wait()
    cos, sin = twiddle[0], twiddle[1]
    spectrum = []
    for tile in range(2):
        real = mixed[:256, tile * 128 : tile * 128 + 128]
        imag = mixed[256:, tile * 128 : tile * 128 + 128]
        turned = jnp.concatenate([real * cos - imag * sin, real * sin + imag * cos], 1)
        spectrum.append(product(split(turned), turner(lane_forward)))
    copies[3].wait()
    wave = waves[...]
    square = wave * wave
    square = square + pltpu.roll(square, 64, 1)
    kept = jnp.where(wave == 64.0, 0.0, 1.0)
    retain = kept * pltpu.roll(kept, 64, 1)
    inverse = 1.0 / jnp.maximum(square + kz * kz, 1.0)
    (hr, hi), (vr, vi) = [(s[:, :128], s[:, 128:]) for s in spectrum]
    flat_r, flat_i = hr * wave, hi * wave
    flat_r = flat_r + pltpu.roll(flat_r, 64, 1)
    flat_i = flat_i + pltpu.roll(flat_i, 64, 1)
    dot_r = (flat_r + kz * vi) * inverse
    dot_i = (flat_i - kz * vr) * inverse
    flat = jnp.concatenate([(hr - wave * dot_r) * retain, (hi - wave * dot_i) * retain], 1)
    upright = jnp.concatenate([(vr + kz * dot_i) * retain, (vi - kz * dot_r) * retain], 1)
    flat, upright = split(flat), split(upright)
    copies[4].wait()
    copies[5].wait()
    cos, sin = twiddle_back[0], twiddle_back[1]
    parts = []
    for component in range(3):
        matrix = lane_backward.at[component % 2]
        cells = product(upright if component == 2 else flat, turner(matrix))
        real, imag = cells[:, :128], cells[:, 128:]
        parts.append(jnp.concatenate([real * cos - imag * sin, real * sin + imag * cos], 0))
    unrow = [jnp.concatenate([row_forward[h, :256], row_forward[h, 256:]], 1) for h in range(2)]
    result = product(unrow, split(jnp.concatenate(parts, 1)))
    for component in range(3):
        block = result[:, component * 128 : component * 128 + 128]
        out[pl.ds(component, 256, stride=3), :] = block


def arrange(
    velocity_far,
    even_far,
    odd_far,
    kernel_in_far,
    kernel_out_far,
    bias_far,
    select_in_far,
    select_out_far,
    select_back_far,
    own,
    even,
    odd,
    bias_rows,
    banded_in,
    banded_out,
    banded_back,
    velocity,
    halo,
    kernel_in,
    kernel_out,
    bias,
    select_in,
    select_out,
    select_back,
    lines_in,
    lines_out,
    sems,
):
    parity = lax.rem(lax.axis_index("px"), 2)
    far = [velocity_far, even_far, odd_far, kernel_in_far, kernel_out_far, bias_far]
    far += [select_in_far, select_out_far, select_back_far]
    near = [velocity, halo.at[1 - parity], halo.at[parity], kernel_in, kernel_out, bias]
    near += [select_in, select_out, select_back]
    for copy in fetch(list(zip(far, near)), sems):
        copy.wait()
    for c in range(3):
        for y in range(4):
            base = (c * 4 + y) * 24
            own[pl.ds(base + 16, 8), :] = jnp.zeros((8, 128), f32)
            own[pl.ds(base, 16), :] = velocity[pl.ds(c * 64 + y, 16, stride=4), :]
            own[pl.ds(base + 16, 3), :] = halo[1, c, :, y, :]
            own[pl.ds(base + 21, 3), :] = halo[0, c, :, y, :]
    parity = lax.rem(lax.axis_index("py"), 2)
    for c in range(3):
        for out, skip in ((even, 1 - parity), (odd, parity)):
            rows = pl.ds(pl.multiple_of((c * 4 + skip) * 24, 8), 72)
            out[pl.ds(c * 72, 72), :] = own[rows, :]
    square = (32, 32)
    diagonal = lax.broadcasted_iota(jnp.int32, square, 0) == lax.broadcasted_iota(
        jnp.int32, square, 1
    )
    column = jnp.sum(jnp.where(diagonal, jnp.broadcast_to(bias[...], square), 0.0), 1, keepdims=True)
    column = jnp.broadcast_to(column, (32, 128))
    for yo in range(6):
        bias_rows[pl.ds(yo * 32, 32), :] = column
    for kernel, lines, count in ((kernel_in, lines_in, 3), (kernel_out, lines_out, 6)):
        for c in range(count):
            for dx in range(3):
                for dy in range(3):
                    rows = pl.ds(((c * 3 + dx) * 3 + dy) * 3, 3)
                    lines[rows, :] = kernel[c, dx, dy].astype(f32)
    lines = lines_in[...].astype(bf16)
    over_rows = (((0,), (0,)), ((), ()))
    for kernel, select, banded in (
        (lines, select_in, banded_in),
        (lines_out[...].astype(bf16), select_out, banded_out),
    ):
        band = lax.dot_general(kernel, select[...], over_rows, preferred_element_type=f32)
        for yo in range(6):
            moved = band
            if yo:
                moved = jnp.concatenate([jnp.zeros((32, yo), f32), band[:, :-yo]], 1)
            banded[pl.ds(yo * 32, 32), :] = moved.astype(bf16)
    band = jnp.dot(select_back[...], lines, preferred_element_type=f32).astype(bf16)
    for block in range(18):
        banded_back[:, pl.ds(block * 32, 32)] = band[block * 48 : block * 48 + 48]


def sixth(at):
    near, middle, far = [at(k) - at(-k) for k in (1, 2, 3)]
    return (45.0 * near - 9.0 * middle + far) * (1.0 / (60.0 * spacing))


def rolled(block, axis):
    return lambda k: pltpu.roll(block, (-k) % block.shape[axis], axis)


def prepare(
    own,
    even,
    odd,
    bias_far,
    banded_in_far,
    field,
    slope,
    slants,
    slabs,
    bias,
    banded_in,
    sems,
):
    pairs = [(bias_far, bias), (banded_in_far, banded_in)]
    parity = lax.rem(lax.axis_index("py"), 2)
    for c in range(3):
        for source, start, rows in (
            (even, 168 * (1 - parity), 72),
            (own, 72, 96),
            (odd, 168 * parity, 72),
        ):
            start = c * 240 + start
            start = start if isinstance(start, int) else pl.multiple_of(start, 8)
            pairs.append((source.at[pl.ds(c * rows, rows), :], field.at[pl.ds(start, rows), :]))
    for copy in fetch(pairs, sems):
        copy.wait()

    lift = jnp.concatenate([bias[...], bias[...]], 1)
    for i in range(20):
        row = (i + 22) % 24
        parts = [field[pl.ds(c * 240 + 24 + row, 8, stride=24), :] for c in range(3)]
        slab = jnp.concatenate(parts, 0)
        shifts = [pltpu.roll(slab, 1, 1), slab, pltpu.roll(slab, 127, 1)]
        slab = jnp.concatenate(shifts + [jnp.zeros((8, 128), f32)], 0).astype(bf16)
        for half, j in enumerate((i, i - 9)):
            if 0 <= j <= 10:
                slabs[pl.ds(j * PRE, PRE), pl.ds(half * 128, 128)] = slab
    for i in range(9):
        cells = slabs[pl.ds(i * PRE, 3 * PRE), :]
        value = jnp.dot(banded_in[...], cells, preferred_element_type=f32) + lift
        value = jnp.tanh(value)
        slope[pl.ds(i * 192, 192), :] = 1.0 - value * value
    for a in range(3):
        for y in range(4):
            base = a * 240 + (y + 3) * 24
            block = field[pl.ds(base, 24), :]
            inner = block[:16]
            along = [
                sixth(rolled(block, 0))[:16],
                sixth(lambda k, base=base: field[pl.ds(base + 24 * k, 16), :]),
                sixth(rolled(inner, 1)),
            ]
            for c in range(3):
                slants[pl.ds(((a * 3 + c) * 4 + y) * 16, 16), :] = along[c]


def finish(
    modes_far,
    table_far,
    field_far,
    slants_far,
    slope_far,
    banded_out_far,
    banded_back_far,
    out,
    modes,
    table,
    field,
    slants,
    slope,
    banded_out,
    banded_back,
    lam,
    stress,
    slabs,
    adjoint,
    closure,
    sems,
):
    copies = fetch(
        [
            (modes_far, modes),
            (table_far, table),
            (field_far, field),
            (slants_far, slants),
            (banded_out_far, banded_out),
            (slope_far, slope),
            (banded_back_far, banded_back),
        ],
        sems,
    )
    copies[0].wait()
    copies[1].wait()
    for c in range(3):
        matrix = table.at[c // 2]
        for part in range(2):
            cells = split(modes[pl.ds(part * 3 + c, 128, stride=6), :])
            values = product(cells, (matrix[0], matrix[1]), (0, 0))
            lam[pl.ds(c * 240 + part * 120, 120), :] = values[:120]
    scale = 1.0 / (2.0 * spacing)
    for y in range(8):
        blocks = [lam[pl.ds(c * 240 + (y + 1) * 24, 24), :] for c in range(3)]
        along_x = [(pltpu.roll(b, 23, 0) - pltpu.roll(b, 1, 0)) * scale for b in blocks]
        along_z = [(pltpu.roll(b, 127, 1) - pltpu.roll(b, 1, 1)) * scale for b in blocks]
        along_y = [
            (lam[pl.ds(c * 240 + (y + 2) * 24, 24), :] - lam[pl.ds(c * 240 + y * 24, 24), :]) * scale
            for c in range(3)
        ]
        values = [
            along_x[0],
            along_y[1],
            along_z[2],
            along_y[0] + along_x[1],
            along_z[0] + along_x[2],
            along_z[1] + along_y[2],
        ]
        for s in range(6):
            stress[pl.ds((s * 8 + y) * 24, 24), :] = values[s]
    for i in range(20):
        slab = stress[pl.ds((i + 22) % 24, 48, stride=24), :]
        shifts = [pltpu.roll(slab, 1, 1), slab, pltpu.roll(slab, 127, 1)]
        slab = jnp.concatenate(shifts, 0).astype(bf16)
        for half, j in enumerate((i, i - 9)):
            if 0 <= j <= 10:
                slabs[pl.ds(j * STR, STR), pl.ds(half * 128, 128)] = slab
    copies[2].wait()
    copies[3].wait()
    for c in range(3):
        across = [
            lam[pl.ds(c * 240 + y * 24, 16), :] * field[pl.ds(240 + y * 24, 16), :]
            for y in range(10)
        ]
        for y in range(4):
            base = (y + 3) * 24
            block = lam[pl.ds(c * 240 + base, 24), :]
            total = sixth(rolled(block * field[pl.ds(base, 24), :], 0))[:16]
            total = total + sixth(lambda k, y=y: across[y + 3 + k])
            total = total + sixth(rolled(block[:16] * field[pl.ds(480 + base, 16), :], 1))
            crossed = [
                lam[pl.ds(a * 240 + base, 16), :] * slants[pl.ds(((a * 3 + c) * 4 + y) * 16, 16), :]
                for a in range(3)
            ]
            total = total - (crossed[0] + crossed[1] + crossed[2])
            out[pl.ds(c * 64 + y, 16, stride=4), :] = block[:16] + time_step * total
    copies[4].wait()
    copies[5].wait()
    for i in range(9):
        cells = slabs[pl.ds(i * STR, 3 * STR), :]
        value = jnp.dot(banded_out[...], cells, preferred_element_type=f32)
        value = (value * slope[pl.ds(i * 192, 192), :]).astype(bf16)
        for x, block in ((i, value[:, :128]), (i + 9, value[:, 128:])):
            for half, j in enumerate((x, x - 8)):
                if 0 <= j <= 9:
                    adjoint[pl.ds(j * 192, 192), pl.ds(half * 128, 128)] = block
    copies[6].wait()
    for i in range(8):
        cells = adjoint[pl.ds(i * 192, 576), :]
        value = jnp.dot(banded_back[...], cells, preferred_element_type=f32)
        for half in range(2):
            block = value[:, half * 128 : half * 128 + 128]
            total = block[16:32] + pltpu.roll(block[:16], 127, 1) + pltpu.roll(block[32:], 1, 1)
            closure[pl.ds((i + 8 * half) * 16, 16), :] = total
    for c in range(3):
        for y in range(4):
            rows = pl.ds(c * 64 + y, 16, stride=4)
            out[rows, :] = out[rows, :] + time_step * closure[pl.ds(c * 4 + y, 16, stride=16), :]


def call(kernel, shapes, args, spaces, outs, scratch=(), copies=0, limit=MOST, flops=0):
    size = 4 * sum(math.prod(s.shape) for s in shapes) + 4 * sum(math.prod(a.shape) for a in args)
    kinds = {"v": pltpu.VMEM, "s": pltpu.SMEM, "h": pltpu.HBM}
    scratch = list(scratch) + ([pltpu.SemaphoreType.DMA((copies,))] if copies else [])
    return pl.pallas_call(
        kernel,
        out_shape=shapes,
        in_specs=[pl.BlockSpec(memory_space=kinds[space]) for space in spaces],
        out_specs=[pl.BlockSpec(memory_space=kinds[space]) for space in outs],
        scratch_shapes=scratch,
        compiler_params=pltpu.CompilerParams(vmem_limit_bytes=limit),
        cost_estimate=pl.CostEstimate(flops=flops, bytes_accessed=size, transcendentals=0),
    )(*args)


def shape(rows, columns=128, kind=f32):
    return jax.ShapeDtypeStruct((rows, columns), kind)


def body(velocity, cotangent, weight_in, bias_in, weight_out):
    t = {name: jnp.asarray(value) for name, value in constants().items()}
    modes, even, odd = call(
        transform_z,
        [shape(512)] + [jax.ShapeDtypeStruct((3, 3, 4, 128), f32)] * 2,
        [cotangent.reshape(192, 128), t["forward_z"], velocity],
        "hhh",
        "vvv",
        [pltpu.VMEM((192, 128), f32), pltpu.VMEM((2, 2, 128, 128), bf16)],
        4,
        flops=4 * 2**22,
    )
    planes = lax.all_to_all(modes.reshape(256, 256), ("px", "py"), 0, 0, tiled=True)
    planes = planes.reshape(512, 128)

    def links(count):
        odd = [(i, (i + 1) % count if i % 2 else (i - 1) % count) for i in range(count)]
        return [(i, i ^ 1) for i in range(count)], odd

    even_links, odd_links = links(PX)
    even = lax.ppermute(even, "px", even_links)
    odd = lax.ppermute(odd, "px", odd_links)
    planes, even, odd = lax.optimization_barrier((planes, even, odd))
    operands = [
        velocity.reshape(192, 128),
        even,
        odd,
        weight_in.transpose(1, 2, 3, 4, 0),
        weight_out.transpose(0, 2, 3, 4, 1),
        bias_in.reshape(1, 32),
        t["select_in"],
        t["select_out"],
        t["select_back"],
    ]
    own, even, odd, bias, banded_in, banded_out, banded_back = call(
        arrange,
        [shape(288), shape(216), shape(216), shape(192)]
        + [shape(192, 3 * PRE, bf16), shape(192, 3 * STR, bf16), shape(48, 576, bf16)],
        operands,
        "h" * 9,
        "v" * 7,
        [pltpu.VMEM((192, 128), f32), pltpu.VMEM((2, 3, 3, 4, 128), f32)]
        + [pltpu.VMEM(a.shape, a.dtype) for a in operands[3:]]
        + [pltpu.VMEM((81, 32), f32), pltpu.VMEM((162, 32), f32)],
        9,
        flops=2**27,
    )
    tables = [
        t["row_forward"],
        t["twiddle"],
        t["lane_forward"],
        t["waves"],
        t["lane_backward"],
        t["twiddle_back"],
    ]
    picked = {4: 1, 5: 1}
    (returned,) = call(
        project,
        [shape(768)],
        [planes] + tables,
        "h" * 7,
        "v",
        [pltpu.VMEM((512, 128), f32)]
        + [pltpu.VMEM(a.shape[picked.get(i, 0) :], a.dtype) for i, a in enumerate(tables)],
        7,
        flops=30 * 2 * 256**3,
    )
    received = lax.all_to_all(returned.reshape(256, 384), ("px", "py"), 0, 0, tiled=True)
    even_links, odd_links = links(PY)
    even = lax.ppermute(even, "py", even_links)
    odd = lax.ppermute(odd, "py", odd_links)
    field, slope, slants = call(
        prepare,
        [shape(720), shape(9 * 192, 256), shape(576)],
        [own, even, odd, bias, banded_in],
        "h" * 5,
        "vvv",
        [
            pltpu.VMEM((11 * PRE, 256), bf16),
            pltpu.VMEM((192, 128), f32),
            pltpu.VMEM((192, 3 * PRE), bf16),
        ],
        11,
        flops=18 * 2 * 192 * 256 * 128,
    )
    operands = [
        received.reshape(768, 128),
        t["backward_z"],
        field,
        slants,
        slope,
        banded_out,
        banded_back,
    ]
    (result,) = call(
        finish,
        [shape(192)],
        operands,
        "h" * 7,
        "v",
        [pltpu.VMEM(a.shape, a.dtype) for a in operands]
        + [
            pltpu.VMEM((720, 128), f32),
            pltpu.VMEM((48 * 24, 128), f32),
            pltpu.VMEM((11 * STR, 256), bf16),
            pltpu.VMEM((10 * 192, 256), bf16),
            pltpu.VMEM((256, 128), f32),
        ],
        7,
        flops=2**29,
    )
    return result.reshape(3, 16, 4, 128)


def solution(mesh):
    placed = (P(None, "px", "py", None), P(None, "px", "py", None), P(), P(), P())
    return jax.shard_map(
        body, mesh=mesh, in_specs=placed, out_specs=P(None, "px", "py", None), check_vma=False
    )
```

```python
import functools
import math

import jax
import jax.numpy as jnp
import ml_dtypes
import numpy as np
from jax import lax
from jax.experimental import pallas as pl
from jax.experimental.pallas import tpu as pltpu
from jax.sharding import PartitionSpec as P

N = 128
PX = 8
PY = 32
time_step = 0.005
spacing = 2.0 * math.pi / N
bf16 = jnp.bfloat16
f32 = jnp.float32
MOST = 2**26 - 2**14
PRE = 80
STR = 144


def halves(table):
    table = np.asarray(table, np.float64)
    high = table.astype(np.float32).astype(ml_dtypes.bfloat16)
    low = (table - high.astype(np.float64)).astype(np.float32).astype(ml_dtypes.bfloat16)
    return np.stack([high, low])


def complex_form(table):
    return np.concatenate([table.real, table.imag], 1)


@functools.cache
def constants():
    z = np.arange(N)
    kz = np.arange(N // 2)
    angle = 2 * np.pi * ((kz[:, None] * z[None]) % N) / N
    cos, sin = np.cos(angle), np.sin(angle)
    weight = np.where(kz == 0, 1.0, 2.0)[:, None] / float(N) ** 3

    def pair(first, second):
        return np.stack([first, second], 1).reshape(N, N)

    forward_z = np.stack([halves(pair(cos, -sin)), halves(pair(sin, cos))])
    backward_z = np.stack(
        [halves(pair(cos * weight, -sin * weight)), halves(pair(sin * weight, cos * weight))]
    )
    a, b = np.arange(PX), np.arange(PY)
    y4, x16 = np.arange(4), np.arange(16)
    phase = a[:, None, None, None] * a[None, None, :, None] / PX
    phase = phase + b[None, :, None, None] * b[None, None, None, :] / PY
    rows = np.exp(-2j * np.pi * phase.reshape(256, 256))
    row_forward = halves(np.concatenate([rows.real, rows.imag], 0))
    phase = a[:, None, None, None] * x16 + b[None, :, None, None] * y4[:, None]
    twiddle = np.exp(-2j * np.pi * phase.reshape(256, 64) / N)
    twiddle = np.tile(twiddle, (1, 2))
    twiddle = np.stack([twiddle.real, twiddle.imag]).astype(np.float32)
    phase = y4[:, None, None, None] * y4[:, None] / 4 + x16[:, None, None] * x16 / 16
    lanes = np.exp(-2j * np.pi * phase.reshape(64, 64))
    lane_forward = halves(complex_form(np.kron(np.eye(2), lanes)))
    m, l = np.broadcast_arrays(
        a[:, None, None, None] + 8 * x16, b[None, :, None, None] + 32 * y4[:, None]
    )
    m, l = m.reshape(256, 64), l.reshape(256, 64)
    kx, ky = np.where(m > 64, m - N, m), np.where(l > 64, l - N, l)
    waves = np.concatenate([kx, ky], 1).astype(np.float32)
    r = np.arange(24)
    xe = np.where(r < 19, r, r - 24)
    lane_backward, twiddle_back = [], []
    for part in range(2):
        ye = np.arange(5) + (5 * part - 3)
        phase = y4[:, None, None, None] * ye[:, None] / 4 + x16[:, None, None] * xe / 16
        table = np.pad(np.exp(2j * np.pi * phase.reshape(64, 120)), ((0, 0), (0, 8)))
        for component in range(2):
            pick = np.eye(2)[:, component : component + 1]
            lane_backward.append(halves(complex_form(np.kron(pick, table))))
        phase = a[:, None, None, None] * xe + b[None, :, None, None] * ye[:, None]
        table = np.pad(np.exp(2j * np.pi * phase.reshape(256, 120) / N), ((0, 0), (0, 8)))
        twiddle_back.append(np.stack([table.real, table.imag]))
    lane_backward = np.stack(lane_backward).reshape(2, 2, 2, 128, 256)
    twiddle_back = np.stack(twiddle_back).astype(np.float32)
    select_in = np.zeros((3, 3, 3, 3, 3 * PRE))
    select_out = np.zeros((6, 3, 3, 3, 3 * STR))
    select_back = np.zeros((3, 6, 3, 16, 3, 3, 3, 3))
    for dx in range(3):
        for dz in range(3):
            for dy in range(3):
                for c in range(3):
                    select_in[c, dx, dy, dz, dx * PRE + dz * 24 + c * 8 + dy] = 1
                for s in range(6):
                    column = dx * STR + dz * 48 + s * 8 + dy
                    select_out[s, 2 - dx, 2 - dy, 2 - dz, column] = 1
            for c in range(3):
                for yo in range(4):
                    for yi in range(6):
                        if 0 <= yo + 2 - yi < 3:
                            select_back[dx, yi, dz, c * 4 + yo, c, 2 - dx, yo + 2 - yi, dz] = 1
    select_in = select_in.reshape(81, 3 * PRE).astype(ml_dtypes.bfloat16)
    select_out = select_out.reshape(162, 3 * STR).astype(ml_dtypes.bfloat16)
    select_back = select_back.reshape(18 * 48, 81).astype(ml_dtypes.bfloat16)
    return dict(
        forward_z=forward_z,
        backward_z=backward_z,
        mixing=np.concatenate([row_forward, lane_forward], 1),
        turning=np.concatenate([twiddle, waves[None]], 0),
        lane_backward=lane_backward,
        twiddle_back=twiddle_back,
        select_in=select_in,
        select_out=select_out,
        select_back=select_back,
    )


def split(value):
    high = value.astype(bf16)
    return high, (value - high.astype(f32)).astype(bf16)


def product(left, right, over=(1, 0)):
    left = jnp.concatenate([left[0], left[1], left[0]], over[0])
    right = jnp.concatenate([right[0], right[0], right[1]], over[1])
    dims = (((over[0],), (over[1],)), ((), ()))
    return lax.dot_general(left, right, dims, preferred_element_type=f32)


def turner(tables):
    whole = []
    for half in range(2):
        top = tables[half]
        bottom = jnp.concatenate([-top[:, 128:], top[:, :128]], 1)
        whole.append(jnp.concatenate([top, bottom], 0))
    return whole


def fetch(pairs, sems, at=0):
    copies = [pltpu.make_async_copy(a, b, sems.at[at + i]) for i, (a, b) in enumerate(pairs)]
    for copy in copies:
        copy.start()
    return copies


def transform_z(source_far, table_far, velocity, out, even, odd, source, table, sems):
    parity = lax.rem(lax.axis_index("px"), 2)
    copies = fetch(
        [
            (source_far, source),
            (table_far, table),
            (velocity.at[:, pl.ds(13 * (1 - parity), 3)], even),
            (velocity.at[:, pl.ds(13 * parity, 3)], odd),
        ],
        sems,
    )
    copies[0].wait()
    copies[1].wait()
    blocks = [[source[pl.ds(c * 64 + y, 16, stride=4), :] for y in range(4)] for c in range(3)]
    flat = jnp.concatenate(blocks[0] + blocks[1], 0)
    upright = jnp.concatenate(blocks[2] + blocks[2], 0)
    for tile, cells in enumerate((flat, upright)):
        modes = product((table[tile, 0], table[tile, 1]), split(cells), (1, 1))
        for copy in range(2):
            out[pl.ds(2 * copy + tile, 128, stride=4), :] = modes
    for copy in copies[2:]:
        copy.wait()


def project(
    source_far,
    mixing_far,
    turning_far,
    lane_backward_far,
    twiddle_back_far,
    out,
    source,
    mixing,
    turning,
    lane_backward,
    twiddle_back,
    sems,
):
    device = lax.axis_index("px") * PY + lax.axis_index("py")
    part = lax.rem(device, 2)
    kz = lax.div(device, 4).astype(f32)
    first, *copies = fetch(
        [
            (source_far, source),
            (mixing_far, mixing),
            (turning_far, turning),
            (lane_backward_far.at[part], lane_backward),
            (twiddle_back_far.at[part], twiddle_back),
        ],
        sems,
    )
    first.wait()
    copies[0].wait()
    tiles = [source[pl.ds(tile, 256, stride=2), :] for tile in range(2)]
    mixed = product((mixing[0, :512], mixing[1, :512]), split(jnp.concatenate(tiles, 1)))
    copies[1].wait()
    cos, sin = turning[0], turning[1]
    spectrum = []
    for tile in range(2):
        real = mixed[:256, tile * 128 : tile * 128 + 128]
        imag = mixed[256:, tile * 128 : tile * 128 + 128]
        turned = jnp.concatenate([real * cos - imag * sin, real * sin + imag * cos], 1)
        spectrum.append(product(split(turned), turner(mixing.at[:, pl.ds(512, 128)])))
    wave = turning[2]
    square = wave * wave
    square = square + pltpu.roll(square, 64, 1)
    kept = jnp.where(wave == 64.0, 0.0, 1.0)
    retain = kept * pltpu.roll(kept, 64, 1)
    inverse = 1.0 / jnp.maximum(square + kz * kz, 1.0)
    (hr, hi), (vr, vi) = [(s[:, :128], s[:, 128:]) for s in spectrum]
    flat_r, flat_i = hr * wave, hi * wave
    flat_r = flat_r + pltpu.roll(flat_r, 64, 1)
    flat_i = flat_i + pltpu.roll(flat_i, 64, 1)
    dot_r = (flat_r + kz * vi) * inverse
    dot_i = (flat_i - kz * vr) * inverse
    flat = jnp.concatenate([(hr - wave * dot_r) * retain, (hi - wave * dot_i) * retain], 1)
    upright = jnp.concatenate([(vr + kz * dot_i) * retain, (vi - kz * dot_r) * retain], 1)
    flat, upright = split(flat), split(upright)
    copies[2].wait()
    copies[3].wait()
    cos, sin = twiddle_back[0], twiddle_back[1]
    parts = []
    for component in range(3):
        matrix = lane_backward.at[component % 2]
        cells = product(upright if component == 2 else flat, turner(matrix))
        real, imag = cells[:, :128], cells[:, 128:]
        parts.append(jnp.concatenate([real * cos - imag * sin, real * sin + imag * cos], 0))
    unrow = [jnp.concatenate([mixing[h, :256], mixing[h, 256:512]], 1) for h in range(2)]
    result = product(unrow, split(jnp.concatenate(parts, 1)))
    for component in range(3):
        block = result[:, component * 128 : component * 128 + 128]
        out[pl.ds(component, 256, stride=3), :] = block


def arrange(velocity_far, even_far, odd_far, own, even, odd, velocity, halo, sems):
    parity = lax.rem(lax.axis_index("px"), 2)
    near = [velocity, halo.at[1 - parity], halo.at[parity]]
    for copy in fetch(list(zip([velocity_far, even_far, odd_far], near)), sems):
        copy.wait()
    for c in range(3):
        for y in range(4):
            base = (c * 4 + y) * 24
            own[pl.ds(base + 16, 8), :] = jnp.zeros((8, 128), f32)
            own[pl.ds(base, 16), :] = velocity[pl.ds(c * 64 + y, 16, stride=4), :]
            own[pl.ds(base + 16, 3), :] = halo[1, c, :, y, :]
            own[pl.ds(base + 21, 3), :] = halo[0, c, :, y, :]
    parity = lax.rem(lax.axis_index("py"), 2)
    for c in range(3):
        for out, skip in ((even, 1 - parity), (odd, parity)):
            rows = pl.ds(pl.multiple_of((c * 4 + skip) * 24, 8), 72)
            out[pl.ds(c * 72, 72), :] = own[rows, :]


def band_weights(
    kernel_in_far,
    kernel_out_far,
    bias_far,
    select_in_far,
    select_out_far,
    select_back_far,
    bias_rows,
    banded_in,
    banded_out,
    banded_back,
    kernel_in,
    kernel_out,
    bias,
    select_in,
    select_out,
    select_back,
    lines_in,
    lines_out,
    sems,
):
    far = [kernel_in_far, kernel_out_far, bias_far, select_in_far, select_out_far, select_back_far]
    near = [kernel_in, kernel_out, bias, select_in, select_out, select_back]
    for copy in fetch(list(zip(far, near)), sems):
        copy.wait()
    square = (32, 32)
    diagonal = lax.broadcasted_iota(jnp.int32, square, 0) == lax.broadcasted_iota(
        jnp.int32, square, 1
    )
    column = jnp.sum(jnp.where(diagonal, jnp.broadcast_to(bias[...], square), 0.0), 1, keepdims=True)
    column = jnp.broadcast_to(column, (32, 128))
    for yo in range(6):
        bias_rows[pl.ds(yo * 32, 32), :] = column
    for kernel, lines, count in ((kernel_in, lines_in, 3), (kernel_out, lines_out, 6)):
        for c in range(count):
            for dx in range(3):
                for dy in range(3):
                    rows = pl.ds(((c * 3 + dx) * 3 + dy) * 3, 3)
                    lines[rows, :] = kernel[c, dx, dy].astype(f32)
    lines = lines_in[...].astype(bf16)
    over_rows = (((0,), (0,)), ((), ()))
    for kernel, select, banded in (
        (lines, select_in, banded_in),
        (lines_out[...].astype(bf16), select_out, banded_out),
    ):
        band = lax.dot_general(kernel, select[...], over_rows, preferred_element_type=f32)
        for yo in range(6):
            moved = band
            if yo:
                moved = jnp.concatenate([jnp.zeros((32, yo), f32), band[:, :-yo]], 1)
            banded[pl.ds(yo * 32, 32), :] = moved.astype(bf16)
    band = jnp.dot(select_back[...], lines, preferred_element_type=f32).astype(bf16)
    for block in range(18):
        banded_back[:, pl.ds(block * 32, 32)] = band[block * 48 : block * 48 + 48]


def sixth(at):
    near, middle, far = [at(k) - at(-k) for k in (1, 2, 3)]
    return (45.0 * near - 9.0 * middle + far) * (1.0 / (60.0 * spacing))


def rolled(block, axis):
    return lambda k: pltpu.roll(block, (-k) % block.shape[axis], axis)


def prepare(
    own,
    even,
    odd,
    bias_far,
    banded_in_far,
    field,
    slope,
    slants,
    slabs,
    bias,
    banded_in,
    sems,
):
    pairs = [(bias_far, bias), (banded_in_far, banded_in)]
    parity = lax.rem(lax.axis_index("py"), 2)
    for c in range(3):
        for source, start, rows in (
            (even, 168 * (1 - parity), 72),
            (own, 72, 96),
            (odd, 168 * parity, 72),
        ):
            start = c * 240 + start
            start = start if isinstance(start, int) else pl.multiple_of(start, 8)
            pairs.append((source.at[pl.ds(c * rows, rows), :], field.at[pl.ds(start, rows), :]))
    for copy in fetch(pairs, sems):
        copy.wait()

    lift = jnp.concatenate([bias[...], bias[...]], 1)
    for i in range(20):
        row = (i + 22) % 24
        parts = [field[pl.ds(c * 240 + 24 + row, 8, stride=24), :] for c in range(3)]
        slab = jnp.concatenate(parts, 0)
        shifts = [pltpu.roll(slab, 1, 1), slab, pltpu.roll(slab, 127, 1)]
        slab = jnp.concatenate(shifts + [jnp.zeros((8, 128), f32)], 0).astype(bf16)
        for half, j in enumerate((i, i - 9)):
            if 0 <= j <= 10:
                slabs[pl.ds(j * PRE, PRE), pl.ds(half * 128, 128)] = slab
    for i in range(9):
        cells = slabs[pl.ds(i * PRE, 3 * PRE), :]
        value = jnp.dot(banded_in[...], cells, preferred_element_type=f32) + lift
        value = jnp.tanh(value)
        slope[pl.ds(i * 192, 192), :] = 1.0 - value * value
    for a in range(3):
        for y in range(4):
            base = a * 240 + (y + 3) * 24
            block = field[pl.ds(base, 24), :]
            inner = block[:16]
            along = [
                sixth(rolled(block, 0))[:16],
                sixth(lambda k, base=base: field[pl.ds(base + 24 * k, 16), :]),
                sixth(rolled(inner, 1)),
            ]
            for c in range(3):
                slants[pl.ds(((a * 3 + c) * 4 + y) * 16, 16), :] = along[c]


def finish(
    modes_far,
    table_far,
    field_far,
    slants_far,
    slope_far,
    banded_out_far,
    banded_back_far,
    out,
    modes,
    table,
    field,
    slants,
    slope,
    banded_out,
    banded_back,
    lam,
    stress,
    slabs,
    adjoint,
    closure,
    sems,
):
    copies = fetch(
        [
            (modes_far, modes),
            (table_far, table),
            (field_far, field),
            (slants_far, slants),
            (banded_out_far, banded_out),
            (slope_far, slope),
            (banded_back_far, banded_back),
        ],
        sems,
    )
    copies[0].wait()
    copies[1].wait()
    for c in range(3):
        matrix = table.at[c // 2]
        for part in range(2):
            cells = split(modes[pl.ds(part * 3 + c, 128, stride=6), :])
            values = product(cells, (matrix[0], matrix[1]), (0, 0))
            lam[pl.ds(c * 240 + part * 120, 120), :] = values[:120]
    scale = 1.0 / (2.0 * spacing)
    for y in range(8):
        blocks = [lam[pl.ds(c * 240 + (y + 1) * 24, 24), :] for c in range(3)]
        along_x = [(pltpu.roll(b, 23, 0) - pltpu.roll(b, 1, 0)) * scale for b in blocks]
        along_z = [(pltpu.roll(b, 127, 1) - pltpu.roll(b, 1, 1)) * scale for b in blocks]
        along_y = [
            (lam[pl.ds(c * 240 + (y + 2) * 24, 24), :] - lam[pl.ds(c * 240 + y * 24, 24), :]) * scale
            for c in range(3)
        ]
        values = [
            along_x[0],
            along_y[1],
            along_z[2],
            along_y[0] + along_x[1],
            along_z[0] + along_x[2],
            along_z[1] + along_y[2],
        ]
        for s in range(6):
            stress[pl.ds((s * 8 + y) * 24, 24), :] = values[s]
    for i in range(20):
        slab = stress[pl.ds((i + 22) % 24, 48, stride=24), :]
        shifts = [pltpu.roll(slab, 1, 1), slab, pltpu.roll(slab, 127, 1)]
        slab = jnp.concatenate(shifts, 0).astype(bf16)
        for half, j in enumerate((i, i - 9)):
            if 0 <= j <= 10:
                slabs[pl.ds(j * STR, STR), pl.ds(half * 128, 128)] = slab
    copies[2].wait()
    copies[3].wait()
    for c in range(3):
        across = [
            lam[pl.ds(c * 240 + y * 24, 16), :] * field[pl.ds(240 + y * 24, 16), :]
            for y in range(10)
        ]
        for y in range(4):
            base = (y + 3) * 24
            block = lam[pl.ds(c * 240 + base, 24), :]
            total = sixth(rolled(block * field[pl.ds(base, 24), :], 0))[:16]
            total = total + sixth(lambda k, y=y: across[y + 3 + k])
            total = total + sixth(rolled(block[:16] * field[pl.ds(480 + base, 16), :], 1))
            crossed = [
                lam[pl.ds(a * 240 + base, 16), :] * slants[pl.ds(((a * 3 + c) * 4 + y) * 16, 16), :]
                for a in range(3)
            ]
            total = total - (crossed[0] + crossed[1] + crossed[2])
            out[pl.ds(c * 64 + y, 16, stride=4), :] = block[:16] + time_step * total
    copies[4].wait()
    copies[5].wait()
    for i in range(9):
        cells = slabs[pl.ds(i * STR, 3 * STR), :]
        value = jnp.dot(banded_out[...], cells, preferred_element_type=f32)
        value = (value * slope[pl.ds(i * 192, 192), :]).astype(bf16)
        for x, block in ((i, value[:, :128]), (i + 9, value[:, 128:])):
            for half, j in enumerate((x, x - 8)):
                if 0 <= j <= 9:
                    adjoint[pl.ds(j * 192, 192), pl.ds(half * 128, 128)] = block
    copies[6].wait()
    for i in range(8):
        cells = adjoint[pl.ds(i * 192, 576), :]
        value = jnp.dot(banded_back[...], cells, preferred_element_type=f32)
        for half in range(2):
            block = value[:, half * 128 : half * 128 + 128]
            total = block[16:32] + pltpu.roll(block[:16], 127, 1) + pltpu.roll(block[32:], 1, 1)
            closure[pl.ds((i + 8 * half) * 16, 16), :] = total
    for c in range(3):
        for y in range(4):
            rows = pl.ds(c * 64 + y, 16, stride=4)
            out[rows, :] = out[rows, :] + time_step * closure[pl.ds(c * 4 + y, 16, stride=16), :]


def call(kernel, shapes, args, spaces, outs, scratch=(), copies=0, limit=MOST, flops=0):
    size = 4 * sum(math.prod(s.shape) for s in shapes) + 4 * sum(math.prod(a.shape) for a in args)
    kinds = {"v": pltpu.VMEM, "s": pltpu.SMEM, "h": pltpu.HBM}
    scratch = list(scratch) + ([pltpu.SemaphoreType.DMA((copies,))] if copies else [])
    return pl.pallas_call(
        kernel,
        out_shape=shapes,
        in_specs=[pl.BlockSpec(memory_space=kinds[space]) for space in spaces],
        out_specs=[pl.BlockSpec(memory_space=kinds[space]) for space in outs],
        scratch_shapes=scratch,
        compiler_params=pltpu.CompilerParams(vmem_limit_bytes=limit),
        cost_estimate=pl.CostEstimate(flops=flops, bytes_accessed=size, transcendentals=0),
    )(*args)


def shape(rows, columns=128, kind=f32):
    return jax.ShapeDtypeStruct((rows, columns), kind)


def body(velocity, cotangent, weight_in, bias_in, weight_out):
    t = {name: jnp.asarray(value) for name, value in constants().items()}
    modes, even, odd = call(
        transform_z,
        [shape(512)] + [jax.ShapeDtypeStruct((3, 3, 4, 128), f32)] * 2,
        [cotangent.reshape(192, 128), t["forward_z"], velocity],
        "hhh",
        "vvv",
        [pltpu.VMEM((192, 128), f32), pltpu.VMEM((2, 2, 128, 128), bf16)],
        4,
        flops=4 * 2**22,
    )
    modes, weight_in, bias_in, weight_out = lax.optimization_barrier(
        (modes, weight_in, bias_in, weight_out)
    )
    planes = lax.all_to_all(modes.reshape(256, 256), ("px", "py"), 0, 0, tiled=True)
    planes = planes.reshape(512, 128)
    operands = [
        weight_in.transpose(1, 2, 3, 4, 0),
        weight_out.transpose(0, 2, 3, 4, 1),
        bias_in.reshape(1, 32),
        t["select_in"],
        t["select_out"],
        t["select_back"],
    ]
    bands = call(
        band_weights,
        [shape(192), shape(192, 3 * PRE, bf16), shape(192, 3 * STR, bf16), shape(48, 576, bf16)],
        operands,
        "h" * 6,
        "v" * 4,
        [pltpu.VMEM(a.shape, a.dtype) for a in operands]
        + [pltpu.VMEM((81, 32), f32), pltpu.VMEM((162, 32), f32)],
        6,
        flops=2**27,
    )

    def links(count):
        odd = [(i, (i + 1) % count if i % 2 else (i - 1) % count) for i in range(count)]
        return [(i, i ^ 1) for i in range(count)], odd

    even_links, odd_links = links(PX)
    even = lax.ppermute(even, "px", even_links)
    odd = lax.ppermute(odd, "px", odd_links)
    planes, even, odd, bands = lax.optimization_barrier((planes, even, odd, bands))
    bias, banded_in, banded_out, banded_back = bands
    own, even, odd = call(
        arrange,
        [shape(288), shape(216), shape(216)],
        [velocity.reshape(192, 128), even, odd],
        "hhh",
        "vvv",
        [pltpu.VMEM((192, 128), f32), pltpu.VMEM((2, 3, 3, 4, 128), f32)],
        3,
        flops=2**24,
    )
    tables = [
        t["mixing"],
        t["turning"],
        t["lane_backward"],
        t["twiddle_back"],
    ]
    picked = {2: 1, 3: 1}
    (returned,) = call(
        project,
        [shape(768)],
        [planes] + tables,
        "h" * 5,
        "v",
        [pltpu.VMEM((512, 128), f32)]
        + [pltpu.VMEM(a.shape[picked.get(i, 0) :], a.dtype) for i, a in enumerate(tables)],
        5,
        flops=30 * 2 * 256**3,
    )
    received = lax.all_to_all(returned.reshape(256, 384), ("px", "py"), 0, 0, tiled=True)
    even_links, odd_links = links(PY)
    even = lax.ppermute(even, "py", even_links)
    odd = lax.ppermute(odd, "py", odd_links)
    field, slope, slants = call(
        prepare,
        [shape(720), shape(9 * 192, 256), shape(576)],
        [own, even, odd, bias, banded_in],
        "h" * 5,
        "vvv",
        [
            pltpu.VMEM((11 * PRE, 256), bf16),
            pltpu.VMEM((192, 128), f32),
            pltpu.VMEM((192, 3 * PRE), bf16),
        ],
        11,
        flops=18 * 2 * 192 * 256 * 128,
    )
    operands = [
        received.reshape(768, 128),
        t["backward_z"],
        field,
        slants,
        slope,
        banded_out,
        banded_back,
    ]
    (result,) = call(
        finish,
        [shape(192)],
        operands,
        "h" * 7,
        "v",
        [pltpu.VMEM(a.shape, a.dtype) for a in operands]
        + [
            pltpu.VMEM((720, 128), f32),
            pltpu.VMEM((48 * 24, 128), f32),
            pltpu.VMEM((11 * STR, 256), bf16),
            pltpu.VMEM((10 * 192, 256), bf16),
            pltpu.VMEM((256, 128), f32),
        ],
        7,
        flops=2**29,
    )
    return result.reshape(3, 16, 4, 128)


def solution(mesh):
    placed = (P(None, "px", "py", None), P(None, "px", "py", None), P(), P(), P())
    return jax.shard_map(
        body, mesh=mesh, in_specs=placed, out_specs=P(None, "px", "py", None), check_vma=False
    )
```
